256 devices in a mesh: req: 64 (over x_lo, z, y), tp: 4 (over x_hi, core).
Axes of the slice: x: 4 (x_hi: 2, x_lo: 2; x = x_hi * 2 + x_lo), y: 4, z: 8, core: 2. Of those that a mesh axis runs over, the one named last changes fastest.
Arguments:
- hidden: bfloat16 [64, 512, 1280], P('req'), may hold values from -6 to 6
- membership: int32 [64], P('req'), may hold values from 0 to 3
- lengths: int32 [64], P('req'), may hold values from 8 to 512, as said below
- owners: int32 [4, 16], replicated, may hold values from 0 to 63, as said below
- prefix_cache: bfloat16 [4096, 20, 128], P('req', 'tp'), may hold values from -6 to 6
- w_query: bfloat16 [1280, 1280], P(None, 'tp'), may hold values from -0.25 to 0.25
- w_key: bfloat16 [1280, 1280], P(None, 'tp'), may hold values from -0.25 to 0.25
- w_value: bfloat16 [1280, 1280], P(None, 'tp'), may hold values from -0.15625 to 0.15625
- key_scale: float32 [20, 64], P('tp'), may hold values from 0.5 to 6
- w_out: bfloat16 [1280, 1280], P('tp'), may hold values from -0.15625 to 0.15625
- step_rates: float32 [1280], replicated, may hold values from 0.1 to 0.8
Outputs:
- layer_out: bfloat16 [64, 512, 1280], P('req', None, 'tp')
The draws below stay inside these ranges and needn't reach their ends.
Inputs may be any that keep to these rules, and one draw needn't show every extreme that they name: `lengths`: every request has at least one suffix token; some request has length 512. `owners`: each cache slot appears exactly once in the table.
All inputs are finite; a program needn't handle non-finite values.
Results may differ from the reference program's by a relative error of at most 0.0085.
Values may be sent and summed in bfloat16 or wider, within the bound.
No kernel may reach another device: no remote copies, remote signals or barrier semaphores. Data moves between devices by JAX's collectives and lax.ppermute only.
A program may use at most 128 MiB of HBM per device.

```python
import math
import jax
import jax.numpy as jnp
from jax import lax

D = 1280
HEADS = 20
HD = 64
SUF = 512
SLOT = 64
GROUPS = 4
SLOTS_G = 16
PREFIX = 1024
REQUESTS = 64
N_REQ = 64
N_TP = 4


def draw_lengths(key, part):
    lowest = max(1, SUF // 64)
    drawn = jax.random.randint(jax.random.fold_in(key, 3), (REQUESTS,), lowest, SUF + 1)
    chosen = jax.random.randint(jax.random.fold_in(key, 5), (), 0, REQUESTS)
    return jnp.where(jnp.arange(REQUESTS) == chosen, SUF, drawn).astype(jnp.int32)


def draw_owners(key, part):
    order = jax.random.permutation(jax.random.fold_in(key, 7), GROUPS * SLOTS_G)
    return order.reshape(GROUPS, SLOTS_G).astype(jnp.int32)


def paired_weights(key):
    fan_scale = D ** (-0.5)
    first_draw = jax.random.normal(jax.random.fold_in(key, 17), (D, HEADS * HD), jnp.float32) * fan_scale
    second_draw = jax.random.normal(jax.random.fold_in(key, 29), (D, HEADS * HD), jnp.float32) * fan_scale
    key_draw = second_draw
    return (jnp.clip(first_draw, -0.25, 0.25), jnp.clip(key_draw, -0.25, 0.25))


def draw_w_query(key, part):
    return paired_weights(key)[0].astype(jnp.bfloat16)


def draw_w_key(key, part):
    return paired_weights(key)[1].astype(jnp.bfloat16)


def draw_key_scale(key, part):
    uniform_draw = jax.random.uniform(jax.random.fold_in(key, 41), (HEADS, HD), jnp.float32)
    lower, upper = (0.5, 2.0)
    return jnp.exp(math.log(lower) + uniform_draw * (math.log(upper) - math.log(lower))).astype(jnp.float32)


def with_ends(array, key, low, top_value):
    spot = [jax.random.randint(jax.random.fold_in(key, axis), (), 0, length) for axis, length in enumerate(array.shape)]
    longest = array.shape.index(max(array.shape))
    neighbour = spot[:longest] + [(spot[longest] + 1) % array.shape[longest]] + spot[longest + 1:]
    return array.at[tuple(spot)].set(low).at[tuple(neighbour)].set(top_value)


def steps_of(own_key, dims, pieces, low, high):
    def one(position, parts):
        draws = jax.random.uniform(jax.random.fold_in(jax.random.fold_in(own_key, 6), position), (parts,), jnp.float32, low / len(pieces), high / len(pieces))
        return jnp.repeat(jnp.exp(draws), dims[position] // parts).reshape((-1,) + (1,) * (len(dims) - position - 1))

    gain = one(*pieces[0])
    for cut in pieces[1:]:
        gain = gain * one(*cut)
    return gain


def normal_values(stream_key, extent, width, reach, pieces=(), kind=jnp.bfloat16):
    entries = width * jax.random.normal(stream_key, extent, jnp.float32)
    if pieces:
        entries = entries * steps_of(stream_key, extent, pieces, -0.22, 0.18)
    return jnp.clip(entries, -reach, reach).astype(kind)


def setup_inputs(seed: int = 0) -> dict:
    splits = jax.random.split(jax.random.key(seed), 12)
    hidden = normal_values(splits[0], (REQUESTS, SUF, D), 1.0, 6.0, ((0, 64),))
    membership = with_ends(jax.random.randint(splits[1], (REQUESTS,), 0, GROUPS), jax.random.fold_in(splits[1], 1), 0, GROUPS - 1).astype(jnp.int32)
    lengths = draw_lengths(jax.random.fold_in(splits[11], 71), 0)
    owners = draw_owners(jax.random.fold_in(splits[11], 71), 0)
    prefix_cache = normal_values(splits[4], (N_REQ * SLOT, HEADS, 2 * HD), 1.0, 6.0, ((0, 64), (1, 4)))
    w_query = draw_w_query(jax.random.fold_in(splits[11], 71), 0)
    w_key = draw_w_key(jax.random.fold_in(splits[11], 71), 0)
    w_value = normal_values(splits[7], (D, HEADS * HD), D ** -0.5, 0.15625, ((1, 4),))
    key_scale = draw_key_scale(jax.random.fold_in(splits[11], 71), 0)
    w_out = normal_values(splits[9], (HEADS * HD, D), (HEADS * HD) ** -0.5, 0.15625, ((0, 4),))
    step_rates = jnp.clip(jnp.exp(jax.random.uniform(splits[10], (D,), jnp.float32, math.log(0.1), math.log(0.8))), 0.1, 0.8)
    return dict(hidden=hidden, membership=membership, lengths=lengths, owners=owners, prefix_cache=prefix_cache, w_query=w_query, w_key=w_key, w_value=w_value, key_scale=key_scale, w_out=w_out, step_rates=step_rates)


def normed(values):
    return values * lax.rsqrt(lax.optimization_barrier(jnp.mean(values * values, axis=-1, keepdims=True)) + 1e-06)

def reference(hidden, membership, lengths, owners, prefix_cache, w_query, w_key, w_value, key_scale, w_out, step_rates):
    per_group = HEADS // N_TP
    slot_table = prefix_cache.reshape(N_REQ, SLOT, HEADS, 2 * HD)[owners]
    slot_table = slot_table.reshape(GROUPS, PREFIX, HEADS, 2 * HD)
    pre_keys = (normed(slot_table[..., :HD].astype(jnp.float32)) * key_scale / math.sqrt(HD)).astype(jnp.bfloat16)
    pre_values = slot_table[..., HD:]
    positions = jnp.arange(SUF)
    causal = positions[None, :] <= positions[:, None]
    out_groups = w_out.reshape(N_TP, per_group * HD, D).astype(jnp.float32)

    def one_request(inputs):
        rows_in, group_one, length_one = inputs
        queries = (normed(jnp.dot(rows_in, w_query, preferred_element_type=jnp.float32).reshape(SUF, HEADS, HD)) * key_scale).astype(jnp.bfloat16)
        key_rows = (normed(jnp.dot(rows_in, w_key, preferred_element_type=jnp.float32).reshape(SUF, HEADS, HD)) * key_scale / math.sqrt(HD)).astype(jnp.bfloat16)
        value_rows = jnp.dot(rows_in, w_value, preferred_element_type=jnp.float32).astype(jnp.bfloat16).reshape(SUF, HEADS, HD)
        all_keys = jnp.concatenate([pre_keys[group_one], key_rows], axis=0).astype(jnp.float32)
        all_values = jnp.concatenate([pre_values[group_one], value_rows], axis=0).astype(jnp.float32)
        visible = jnp.concatenate([jnp.ones((SUF, PREFIX), bool), causal & (positions[None, :] < length_one)], axis=1)
        scores = jnp.einsum('qhd,khd->hqk', queries.astype(jnp.float32), all_keys)
        masked = jnp.where(visible[None], scores, -1e+30)
        row_peak = lax.optimization_barrier(jnp.max(masked, axis=-1, keepdims=True))
        weights = jnp.where(visible[None], jnp.exp(masked - row_peak), 0.0)
        row_sum = lax.optimization_barrier(jnp.sum(weights, axis=-1))
        rounded = lax.optimization_barrier(weights.astype(jnp.bfloat16)).astype(jnp.float32)
        attended = jnp.einsum('hqk,khd->hqd', rounded, all_values) / row_sum[..., None]
        attended = attended.transpose(1, 0, 2).reshape(SUF, HEADS * HD).astype(jnp.bfloat16)
        grouped = attended.reshape(SUF, N_TP, per_group * HD).astype(jnp.float32)
        branch_parts = jnp.einsum('snc,ncd->nsd', grouped, out_groups)
        branch_parts = lax.optimization_barrier(branch_parts.astype(jnp.bfloat16)).astype(jnp.float32)
        branch = normed(lax.optimization_barrier(jnp.sum(branch_parts, axis=0)))
        state_rows = rows_in.astype(jnp.float32)
        updated = normed(state_rows + step_rates * (branch - state_rows))
        valid = (positions < length_one)[:, None]
        return jnp.where(valid, updated, 0.0).astype(jnp.bfloat16)
    return lax.map(one_request, (hidden, membership, lengths))
```

```python
import math

import jax
import jax.numpy as jnp
import numpy as np
from jax import lax
from jax.experimental import pallas as pl
from jax.experimental.pallas import tpu as pltpu
from jax.sharding import PartitionSpec as P

F32 = jnp.float32
BF16 = jnp.bfloat16
LOG2E = math.log2(math.e)
EPS = 1e-06

NX, NZ, NY = 2, 8, 4


def add3(a, b):
    return ((a[0] + b[0]) % NX, (a[1] + b[1]) % NZ, (a[2] + b[2]) % NY)


def flat3(a):
    return a[0] * NZ * NY + a[1] * NY + a[2]


def unflat3(i):
    return (i // (NZ * NY), (i // NY) % NZ, i % NY)


def fetch(array, offset):
    pairs = [(flat3(add3(unflat3(i), offset)), i) for i in range(NX * NZ * NY)]
    return lax.ppermute(array, "req", pairs)


HALVES = (
    dict(
        quad=((0, 0, 0), (1, 0, 2), (0, 4, 0), (1, 4, 2)),
        pool=((0, 0, 0), (0, 1, 0), (0, 7, 0), (0, 2, 0)),
        near=((0, 0, 1), (0, 0, 3), (1, 0, 0), (0, 0, 2)),
    ),
    dict(
        quad=((0, 0, 0), (1, 2, 0), (0, 4, 0), (1, 6, 0)),
        pool=((0, 0, 0), (0, 0, 1), (0, 0, 3), (0, 0, 2)),
        near=((0, 1, 0), (0, 7, 0), (1, 0, 0), (0, 2, 0)),
    ),
)
SPLIT = 3


def place_table(half):
    quads = [[add3(p, q) for q in half["quad"]] for p in half["pool"]]
    plus, minus, across, two = half["near"]
    order = [m for quad in quads for m in quad]
    order += [add3(plus, m) for quad in quads for m in quad]
    order += [add3(minus, m) for quad in quads for m in quad]
    order += [add3(across, m) for quad in quads[:SPLIT] for m in quad]
    order += [add3(two, m) for quad in quads[SPLIT:] for m in quad]
    assert sorted(flat3(m) for m in order) == list(range(64))
    table = np.zeros(64, np.int32)
    for place, m in enumerate(order):
        table[flat3(m)] = place
    return table


def dot_t(a, b):
    return lax.dot_general(a, b, (((1,), (1,)), ((), ())), preferred_element_type=F32)


def qkv_kernel(hid_ref, wq_ref, wk_ref, wv_ref, scale_ref, q_ref, kv_ref):
    heads = q_ref.shape[0]
    size = scale_ref.shape[1] // heads
    rows = hid_ref[...]
    q = jnp.dot(rows, wq_ref[...], preferred_element_type=F32)
    k = jnp.dot(rows, wk_ref[...], preferred_element_type=F32)
    v = jnp.dot(rows, wv_ref[...], preferred_element_type=F32)
    for h in range(heads):
        cols = slice(h * size, (h + 1) * size)
        scale = scale_ref[:, cols]
        qh, kh = q[:, cols], k[:, cols]
        qr = lax.rsqrt(jnp.mean(qh * qh, axis=-1, keepdims=True) + EPS)
        kr = lax.rsqrt(jnp.mean(kh * kh, axis=-1, keepdims=True) + EPS)
        qn = qh * qr * (scale * (LOG2E / math.sqrt(size)))
        q_ref[h] = jnp.concatenate([qn, jnp.zeros_like(qn)], axis=1).astype(BF16)
        kv_ref[h] = jnp.concatenate([kh * kr * scale, v[:, cols]], axis=1).astype(BF16)


def suffix_kernel(len_ref, q_ref, kv_ref, acc_ref, peak_ref, *, tile):
    heads, suf, lanes = q_ref.shape
    size = lanes // 2
    length = len_ref[0]
    lane = lax.broadcasted_iota(jnp.int32, (1, lanes), 1)
    for i in range(suf // tile):
        rows = slice(i * tile, (i + 1) * tile)
        count = (i + 1) * tile
        qpos = lax.broadcasted_iota(jnp.int32, (tile, count), 0) + i * tile
        kpos = lax.broadcasted_iota(jnp.int32, (tile, count), 1)
        visible = (kpos <= qpos) & (kpos < length)
        peaks = jnp.zeros((tile, lanes), F32)
        for h in range(heads):
            keys = kv_ref[h, :count]
            ones_values = jnp.where(lane < size, jnp.ones_like(keys), keys)
            scores = jnp.where(visible, dot_t(q_ref[h, rows], keys), -1e30)
            peak = jnp.max(scores, axis=-1, keepdims=True)
            weights = jnp.exp2(scores - peak).astype(BF16)
            acc_ref[h, rows] = jnp.dot(weights, ones_values, preferred_element_type=F32)
            peaks = jnp.where(lane == h, peak, peaks)
        peak_ref[rows] = peaks


def prefix_kernel(
    member_ref, place_ref, owners_ref, table_ref,
    q_ref, acc_ref, peak_ref, scale_ref, *rest, tile,
):
    blocks = (rest[:5], rest[5:10])
    out_ref, kv_ref, sems = rest[10:]
    heads, suf, lanes = q_ref.shape
    size = lanes // 2
    group = member_ref[0]
    me = place_ref[0]
    slots = owners_ref.shape[1]
    part = kv_ref.shape[1] // (2 * slots)
    bounds = (0, 16, 32, 48, 48 + 4 * SPLIT, 64)
    for j in range(slots):
        owner = owners_ref[group, j]
        rel = (
            ((owner ^ me) & 32)
            + ((((owner >> 2) - (me >> 2)) & 7) << 2)
            + ((owner - me) & 3)
        )
        for half in range(2):
            place = table_ref[half * 64 + rel]
            goal = kv_ref.at[:, pl.ds((2 * j + half) * part, part), :]
            for n, ref in enumerate(blocks[half]):
                low, high = bounds[n], bounds[n + 1]

                @pl.when((place >= low) & (place < high))
                def _(ref=ref, low=low, goal=goal, place=place, sem=sems.at[2 * j + half]):
                    pltpu.make_async_copy(ref.at[place - low], goal, sem).start()

    for j in range(2 * slots):
        goal = kv_ref.at[:, pl.ds(j * part, part), :]
        pltpu.make_async_copy(blocks[0][0].at[0], goal, sems.at[j]).wait()
    lane = lax.broadcasted_iota(jnp.int32, (1, lanes), 1)
    first = lane < size
    odd = None
    for h in range(heads):
        raw = kv_ref[h]
        wide = raw.astype(F32)
        mean = jnp.sum(jnp.where(first, wide * wide, 0.0), axis=-1, keepdims=True) * (1.0 / size)
        keys = (wide * lax.rsqrt(mean + EPS) * scale_ref[h : h + 1]).astype(BF16)
        ones_values = jnp.where(first, jnp.ones_like(raw), raw)
        for i in range(suf // tile):
            rows = slice(i * tile, (i + 1) * tile)
            scores = dot_t(q_ref[h, rows], keys)
            near_peak = peak_ref[rows, h : h + 1]
            peak = jnp.maximum(jnp.max(scores, axis=-1, keepdims=True), near_peak)
            weights = jnp.exp2(scores - peak).astype(BF16)
            total = jnp.dot(weights, ones_values, preferred_element_type=F32)
            total = total + acc_ref[h, rows] * jnp.exp2(near_peak - peak)
            value = total[:, size:] / total[:, :size]
            out_ref[rows, h * size : (h + 1) * size] = value.astype(BF16)


def output_kernel(
    len_ref, rank_ref, a0, a1, a2, a3, w0, w1, w2, w3, hid_ref, rate_ref, out_ref, *, tile
):
    suf, width = hid_ref.shape
    part = out_ref.shape[1]
    length = len_ref[0]
    rank = rank_ref[0]
    rates = rate_ref[...]
    for i in range(suf // tile):
        rows = slice(i * tile, (i + 1) * tile)
        branch = jnp.dot(a0[rows], w0[...], preferred_element_type=F32)
        for a, w in ((a1, w1), (a2, w2), (a3, w3)):
            branch += jnp.dot(a[rows], w[...], preferred_element_type=F32)
        branch = branch * lax.rsqrt(jnp.mean(branch * branch, axis=-1, keepdims=True) + EPS)
        state = hid_ref[rows].astype(F32)
        moved = state + rates * (branch - state)
        norm = lax.rsqrt(jnp.mean(moved * moved, axis=-1, keepdims=True) + EPS)
        pos = lax.broadcasted_iota(jnp.int32, (tile, 1), 0) + i * tile
        result = jnp.where(pos < length, moved * norm, 0.0).astype(BF16)
        for t in range(width // part):

            @pl.when(rank == t)
            def _(t=t, result=result, rows=rows):
                out_ref[rows] = result[:, t * part : (t + 1) * part]


VMEM = pl.BlockSpec(memory_space=pltpu.VMEM)
SMEM = pl.BlockSpec(memory_space=pltpu.SMEM)
ANY = pl.BlockSpec(memory_space=pl.ANY)


def across(array, bit):
    return lax.ppermute(array, "tp", [(i, i ^ bit) for i in range(4)])


def gather_pools(prefix_cache):
    blocks = jnp.transpose(prefix_cache, (1, 0, 2))
    heads, rows, lanes = blocks.shape
    part = rows // 2
    whole_far = fetch(blocks, (0, 4, 0))
    pools = []
    for n, half in enumerate(HALVES):
        cut = slice(n * part, (n + 1) * part)
        mine, far = blocks[:, cut], whole_far[:, cut]
        quad = jnp.stack([mine, fetch(mine, half["quad"][1]), far, fetch(mine, half["quad"][3])])
        pools.append([quad])
    for held, half in zip(pools, HALVES):
        held += [fetch(held[0], offset) for offset in half["pool"][1:]]
    result = []
    for held, half in zip(pools, HALVES):
        plus, minus, across_x, two = half["near"]
        pool = jnp.concatenate(held)
        result.append(
            (
                pool,
                fetch(pool, plus),
                fetch(pool, minus),
                fetch(pool[: 4 * SPLIT], across_x),
                fetch(pool[4 * SPLIT :], two),
            )
        )
    return result


def local(
    hidden,
    membership,
    lengths,
    owners,
    prefix_cache,
    w_query,
    w_key,
    w_value,
    key_scale,
    w_out,
    step_rates,
):
    _, suf, width = hidden.shape
    heads, size = key_scale.shape
    rows = hidden.reshape(suf, width)
    pools = gather_pools(prefix_cache)
    w_far = across(w_out, 2)
    w_core = across(w_out, 1)
    w_both = across(w_far, 1)
    q, kv = pl.pallas_call(
        qkv_kernel,
        out_shape=(jax.ShapeDtypeStruct((heads, suf, 2 * size), BF16),) * 2,
        in_specs=[VMEM] * 5,
        out_specs=(VMEM, VMEM),
        name="qkv",
        cost_estimate=pl.CostEstimate(
            flops=2 * suf * width * 3 * heads * size, transcendentals=0, bytes_accessed=5_000_000
        ),
    )(rows, w_query, w_key, w_value, key_scale.reshape(1, heads * size))

    def suffix_part(length, q, kv, *, tile=128):
        return pl.pallas_call(
            lambda *refs: suffix_kernel(*refs, tile=tile),
            out_shape=(
                jax.ShapeDtypeStruct((heads, suf, 2 * size), F32),
                jax.ShapeDtypeStruct((suf, 2 * size), F32),
            ),
            in_specs=[SMEM, VMEM, VMEM],
            out_specs=(VMEM, VMEM),
            name="suffix",
            cost_estimate=pl.CostEstimate(
                flops=4 * suf * suf * heads * 2 * size,
                transcendentals=suf * suf * heads,
                bytes_accessed=5_000_000,
            ),
        )(length, q, kv)

    acc, peaks = suffix_part(lengths, q, kv)
    table = jnp.asarray(np.concatenate([place_table(half) for half in HALVES]))
    place = lax.axis_index("req").astype(jnp.int32).reshape(1)
    scale = jnp.concatenate([key_scale, jnp.ones_like(key_scale)], axis=1)
    prefix_rows = owners.shape[1] * prefix_cache.shape[0]
    attended = pl.pallas_call(
        lambda *refs: prefix_kernel(*refs, tile=128),
        out_shape=jax.ShapeDtypeStruct((suf, heads * size), BF16),
        in_specs=[SMEM] * 4 + [VMEM] * 4 + [ANY] * 10,
        out_specs=VMEM,
        scratch_shapes=[
            pltpu.VMEM((heads, prefix_rows, 2 * size), BF16),
            pltpu.SemaphoreType.DMA((2 * owners.shape[1],)),
        ],
        name="prefix",
        cost_estimate=pl.CostEstimate(
            flops=4 * suf * prefix_rows * heads * 2 * size,
            transcendentals=suf * prefix_rows * heads,
            bytes_accessed=5_000_000,
        ),
    )(membership, place, owners, table, q, acc, peaks, scale, *pools[0], *pools[1])
    far = across(attended, 2)
    core = across(attended, 1)
    both = across(far, 1)
    part = width // 4
    rank = lax.axis_index("tp").astype(jnp.int32).reshape(1)
    layer_out = pl.pallas_call(
        lambda *refs: output_kernel(*refs, tile=128),
        out_shape=jax.ShapeDtypeStruct((suf, part), BF16),
        in_specs=[SMEM] * 2 + [VMEM] * 10,
        out_specs=VMEM,
        name="output",
        cost_estimate=pl.CostEstimate(
            flops=2 * suf * width * width, transcendentals=0, bytes_accessed=6_000_000
        ),
    )(lengths, rank, attended, core, far, both, w_out, w_core, w_far, w_both, rows, step_rates.reshape(1, width))
    return layer_out.reshape(1, suf, part)


def solution(mesh):
    in_specs = (
        P("req", None, None),
        P("req"),
        P("req"),
        P(),
        P("req", "tp", None),
        P(None, "tp"),
        P(None, "tp"),
        P(None, "tp"),
        P("tp", None),
        P("tp", None),
        P(),
    )
    out_specs = P("req", None, "tp")
    return jax.shard_map(local, mesh=mesh, in_specs=in_specs, out_specs=out_specs, check_vma=False)
```

```python
import math

import jax
import jax.numpy as jnp
import numpy as np
from jax import lax
from jax.experimental import pallas as pl
from jax.experimental.pallas import tpu as pltpu
from jax.sharding import PartitionSpec as P

F32 = jnp.float32
BF16 = jnp.bfloat16
LOG2E = math.log2(math.e)
EPS = 1e-06

NX, NZ, NY = 2, 8, 4


def add3(a, b):
    return ((a[0] + b[0]) % NX, (a[1] + b[1]) % NZ, (a[2] + b[2]) % NY)


def flat3(a):
    return a[0] * NZ * NY + a[1] * NY + a[2]


def unflat3(i):
    return (i // (NZ * NY), (i // NY) % NZ, i % NY)


def fetch(array, offset):
    pairs = [(flat3(add3(unflat3(i), offset)), i) for i in range(NX * NZ * NY)]
    return lax.ppermute(array, "req", pairs)


HALVES = (
    dict(
        quad=((0, 0, 0), (0, 4, 0), (1, 0, 2), (1, 4, 2)),
        pool=((0, 0, 0), (0, 1, 0), (0, 7, 0), (0, 2, 0)),
        near=((0, 0, 1), (0, 0, 3), (1, 0, 0), (0, 0, 2)),
    ),
    dict(
        quad=((0, 0, 0), (0, 4, 0), (1, 2, 0), (1, 6, 0)),
        pool=((0, 0, 0), (0, 0, 1), (0, 0, 3), (0, 0, 2)),
        near=((0, 1, 0), (0, 7, 0), (1, 0, 0), (0, 2, 0)),
    ),
)
CHUNKS = 2
SPLIT = 3


def place_table(half):
    quads = [[add3(p, q) for q in half["quad"]] for p in half["pool"]]
    plus, minus, across, two = half["near"]
    order = [m for quad in quads for m in quad]
    order += [add3(plus, m) for quad in quads for m in quad]
    order += [add3(minus, m) for quad in quads for m in quad]
    order += [add3(across, m) for quad in quads[:SPLIT] for m in quad]
    order += [add3(two, m) for quad in quads[SPLIT:] for m in quad]
    assert sorted(flat3(m) for m in order) == list(range(64))
    table = np.zeros(64, np.int32)
    for place, m in enumerate(order):
        table[flat3(m)] = place
    return table


def dot_t(a, b):
    return lax.dot_general(a, b, (((1,), (1,)), ((), ())), preferred_element_type=F32)


def pair_lanes(scale, fill):
    return jnp.concatenate([scale, jnp.full_like(scale, fill)], axis=1)


def lane_half(lanes):
    return lax.broadcasted_iota(jnp.int32, (1, lanes), 1) < lanes // 2


def prep_kernel(block_ref, scale_ref, flag_ref, whole_ref, one_ref, two_ref):
    heads, rows, lanes = block_ref.shape
    size = lanes // 2
    first = lane_half(lanes)
    scale = scale_ref[...]
    bound = jnp.max(scale * scale) * (1.02 * LOG2E * math.sqrt(size))
    flag_ref[0] = (bound <= 60.0).astype(jnp.int32)
    for h in range(heads):
        wide = block_ref[h].astype(F32)
        mean = jnp.sum(jnp.where(first, wide * wide, 0.0), axis=-1, keepdims=True) * (1.0 / size)
        keys = wide * lax.rsqrt(mean + EPS) * pair_lanes(scale[h : h + 1], 1.0)
        block = jnp.where(first, keys, wide).astype(BF16)
        whole_ref[h] = block
        one_ref[h] = block[: rows // 2]
        two_ref[h] = block[rows // 2 :]


def qkv_kernel(hid_ref, wq_ref, wk_ref, wv_ref, scale_ref, q_ref, kv_ref, w_ref, *, tile):
    heads, suf, lanes = q_ref.shape
    size = lanes // 2
    first = lane_half(lanes)
    for h in range(heads):
        own = slice(h * size, (h + 1) * size)
        w_ref[h, :size] = wq_ref[own]
        w_ref[h, size : 2 * size] = jnp.zeros_like(wq_ref[own])
        w_ref[h, 2 * size : 3 * size] = wk_ref[own]
        w_ref[h, 3 * size :] = wv_ref[own]
    for h in range(heads):
        scale = scale_ref[h : h + 1]
        q_scale = pair_lanes(scale * (LOG2E / math.sqrt(size)), 0.0)
        k_scale = pair_lanes(scale, 1.0)
        for i in range(suf // tile):
            rows = slice(i * tile, (i + 1) * tile)
            both = dot_t(hid_ref[rows], w_ref[h])
            q, kv = both[:, :lanes], both[:, lanes:]
            q_mean = jnp.sum(q * q, axis=-1, keepdims=True) * (1.0 / size)
            k_mean = jnp.sum(jnp.where(first, kv * kv, 0.0), axis=-1, keepdims=True) * (1.0 / size)
            q_ref[h, rows] = (q * lax.rsqrt(q_mean + EPS) * q_scale).astype(BF16)
            keys = kv * lax.rsqrt(k_mean + EPS) * k_scale
            kv_ref[h, rows] = jnp.where(first, keys, kv).astype(BF16)


def suffix_kernel(len_ref, flag_ref, q_ref, kv_ref, acc_ref, peak_ref, *, tile):
    heads, suf, lanes = q_ref.shape
    first = lane_half(lanes)
    length = len_ref[0]
    safe = flag_ref[0] == 1

    @pl.when(safe)
    def _():
        qpos = lax.broadcasted_iota(jnp.int32, (tile, tile), 0)
        kpos = lax.broadcasted_iota(jnp.int32, (tile, tile), 1)
        masks = []
        for j in range(suf // tile):
            inside = kpos + j * tile < length
            masks.append((inside & (kpos <= qpos), inside))
        for h in range(heads):
            for i in range(suf // tile):
                rows = slice(i * tile, (i + 1) * tile)
                total = None
                for j in range(i + 1):
                    keys = kv_ref[h, j * tile : (j + 1) * tile]
                    weights = jnp.exp2(dot_t(q_ref[h, rows], keys))
                    weights = jnp.where(masks[j][0 if i == j else 1], weights, 0.0).astype(BF16)
                    ones_values = jnp.where(first, jnp.ones_like(keys), keys)
                    part = jnp.dot(weights, ones_values, preferred_element_type=F32)
                    total = part if total is None else total + part
                acc_ref[h, rows] = total

    @pl.when(jnp.logical_not(safe))
    def _():
        lane = lax.broadcasted_iota(jnp.int32, (1, lanes), 1)
        peak_ref[...] = jnp.zeros_like(peak_ref)

        def head(h, carry):
            for i in range(suf // tile):
                rows = slice(i * tile, (i + 1) * tile)
                count = (i + 1) * tile
                qpos = lax.broadcasted_iota(jnp.int32, (tile, count), 0) + i * tile
                kpos = lax.broadcasted_iota(jnp.int32, (tile, count), 1)
                keys = kv_ref[h, :count]
                scores = jnp.where(
                    (kpos <= qpos) & (kpos < length), dot_t(q_ref[h, rows], keys), -1e30
                )
                peak = jnp.max(scores, axis=-1, keepdims=True)
                weights = jnp.exp2(scores - peak).astype(BF16)
                ones_values = jnp.where(first, jnp.ones_like(keys), keys)
                acc_ref[h, rows] = jnp.dot(weights, ones_values, preferred_element_type=F32)
                peak_ref[rows] = jnp.where(lane == h, peak, peak_ref[rows])
            return carry

        lax.fori_loop(0, heads, head, 0)


def pack_kernel(a_ref, b_ref, c_ref, d_ref, pool_ref, head_ref):
    for n, ref in enumerate((a_ref, b_ref, c_ref, d_ref)):
        block = ref[...]
        pool_ref[4 * n : 4 * n + 4] = block
        if n < SPLIT:
            head_ref[4 * n : 4 * n + 4] = block


def select_kernel(member_ref, place_ref, owners_ref, table_ref, *rest):
    blocks = (rest[:5], rest[5:10])
    kv_ref, sems = rest[10:]
    group = member_ref[0]
    me = place_ref[0]
    slots = owners_ref.shape[1]
    part = kv_ref.shape[1] // (2 * slots)
    bounds = (0, 16, 32, 48, 48 + 4 * SPLIT, 64)

    def start(j, carry):
        owner = owners_ref[group, j]
        rel = (
            ((owner ^ me) & 32)
            + ((((owner >> 2) - (me >> 2)) & 7) << 2)
            + ((owner - me) & 3)
        )
        for half in range(2):
            place = table_ref[half * 64 + rel]
            row = pl.multiple_of((2 * j + half) * part, part)
            goal = kv_ref.at[:, pl.ds(row, part), :]
            for n, ref in enumerate(blocks[half]):
                low, high = bounds[n], bounds[n + 1]

                @pl.when((place >= low) & (place < high))
                def _(ref=ref, low=low):
                    pltpu.make_async_copy(ref.at[place - low], goal, sems.at[2 * j + half]).start()

        return carry

    lax.fori_loop(0, slots, start, 0)

    def finish(j, carry):
        row = pl.multiple_of(j * part, part)
        goal = kv_ref.at[:, pl.ds(row, part), :]
        pltpu.make_async_copy(blocks[0][0].at[0], goal, sems.at[j]).wait()
        return carry

    lax.fori_loop(0, 2 * slots, finish, 0)


def attend_kernel(flag_ref, q_ref, acc_ref, peak_ref, kv_ref, out_ref, total_ref, *, tile):
    heads, rows, lanes = q_ref.shape
    size = lanes // 2
    count = kv_ref.shape[1]
    first = lane_half(lanes)
    safe = flag_ref[0] == 1

    @pl.when(safe)
    def _():
        for h in range(heads):
            total = acc_ref[h]
            for j in range(count // tile):
                keys = kv_ref[h, j * tile : (j + 1) * tile]
                weights = jnp.exp2(dot_t(q_ref[h], keys)).astype(BF16)
                ones_values = jnp.where(first, jnp.ones_like(keys), keys)
                total = total + jnp.dot(weights, ones_values, preferred_element_type=F32)
            total_ref[h] = total

    @pl.when(jnp.logical_not(safe))
    def _():
        lane = lax.broadcasted_iota(jnp.int32, (1, lanes), 1)

        def head(h, carry):
            keys = kv_ref[h]
            scores = dot_t(q_ref[h], keys)
            near = jnp.max(jnp.where(lane == h, peak_ref[...], -3e38), axis=-1, keepdims=True)
            peak = jnp.maximum(jnp.max(scores, axis=-1, keepdims=True), near)
            weights = jnp.exp2(scores - peak).astype(BF16)
            ones_values = jnp.where(first, jnp.ones_like(keys), keys)
            total = jnp.dot(weights, ones_values, preferred_element_type=F32)
            total_ref[h] = total + acc_ref[h] * jnp.exp2(near - peak)
            return carry

        lax.fori_loop(0, heads, head, 0)

    for h in range(heads):
        total = total_ref[h]
        value = total / pltpu.roll(total, size, 1)
        out_ref[:, h * size : (h + 1) * size] = value[:, size:].astype(BF16)


def output_kernel(
    len_ref, rank_ref, a0, a1, a2, a3, w0, w1, w2, w3, hid_ref, rate_ref, *rest, tile, start
):
    out_ref = rest[-1]
    count, width = hid_ref.shape
    part = out_ref.shape[0]
    length = len_ref[0]
    rank = rank_ref[0]
    rates = rate_ref[...]
    for i in range(count // tile):
        rows = slice(i * tile, (i + 1) * tile)
        branch = jnp.dot(a0[rows], w0[...], preferred_element_type=F32)
        for a, w in ((a1, w1), (a2, w2), (a3, w3)):
            branch += jnp.dot(a[rows], w[...], preferred_element_type=F32)
        branch = branch * lax.rsqrt(jnp.mean(branch * branch, axis=-1, keepdims=True) + EPS)
        state = hid_ref[rows].astype(F32)
        moved = state + rates * (branch - state)
        norm = lax.rsqrt(jnp.mean(moved * moved, axis=-1, keepdims=True) + EPS)
        pos = lax.broadcasted_iota(jnp.int32, (tile, 1), 0) + (i * tile + start)
        result = jnp.where(pos < length, moved * norm, 0.0)
        for t in range(width // part):

            @pl.when(rank == t)
            def _(t=t, result=result, rows=rows):
                out_ref[:, rows] = result[:, t * part : (t + 1) * part].T.astype(BF16)


VMEM = pl.BlockSpec(memory_space=pltpu.VMEM)
SMEM = pl.BlockSpec(memory_space=pltpu.SMEM)
ANY = pl.BlockSpec(memory_space=pl.ANY)


def across(array, bit):
    return lax.ppermute(array, "tp", [(i, i ^ bit) for i in range(4)])


def shaped(shape, dtype):
    return jax.ShapeDtypeStruct(shape, dtype)


def cost(flops, exps, moved):
    return pl.CostEstimate(flops=flops, transcendentals=exps, bytes_accessed=moved)


def gather_pools(whole, halves):
    far = fetch(whole, (0, 4, 0))
    part = whole.shape[1] // 2
    quads = []
    for n, (half, mine) in enumerate(zip(HALVES, halves)):
        pair = jnp.stack([mine, far[:, n * part : (n + 1) * part]])
        quads.append(jnp.concatenate([pair, fetch(pair, half["quad"][2])]))
    held = [
        [quad] + [fetch(quad, offset) for offset in half["pool"][1:]]
        for quad, half in zip(quads, HALVES)
    ]
    result = []
    for (a, b, c, d), half in zip(held, HALVES):
        plus, minus, across_x, two = half["near"]
        shape = a.shape[1:]
        pool, head = pl.pallas_call(
            pack_kernel,
            out_shape=(shaped((16,) + shape, BF16), shaped((4 * SPLIT,) + shape, BF16)),
            in_specs=[VMEM] * 4,
            out_specs=(VMEM, VMEM),
            name="pack",
            cost_estimate=cost(0, 0, 4_000_000),
        )(a, b, c, d)
        result.append(
            (pool, fetch(pool, plus), fetch(pool, minus), fetch(head, across_x), fetch(d, two))
        )
    return result


def local(
    hidden,
    membership,
    lengths,
    owners,
    prefix_cache,
    w_query,
    w_key,
    w_value,
    key_scale,
    w_out,
    step_rates,
):
    _, suf, width = hidden.shape
    heads, size = key_scale.shape
    lanes = 2 * size
    slot_rows = prefix_cache.shape[0]
    rows = hidden.reshape(suf, width)
    block = (heads, slot_rows, lanes)
    half_block = (heads, slot_rows // 2, lanes)
    flag, whole, one, two = pl.pallas_call(
        prep_kernel,
        out_shape=(
            shaped((1,), jnp.int32), shaped(block, BF16), shaped(half_block, BF16), shaped(half_block, BF16),
        ),
        in_specs=[VMEM, VMEM],
        out_specs=(SMEM, VMEM, VMEM, VMEM),
        name="prep",
        cost_estimate=cost(0, 0, 300_000),
    )(jnp.transpose(prefix_cache, (1, 0, 2)), key_scale)
    pools = gather_pools(whole, (one, two))
    w_far = across(w_out, 2)
    w_core = across(w_out, 1)
    w_both = across(w_far, 1)
    q, kv = pl.pallas_call(
        lambda *refs: qkv_kernel(*refs, tile=256),
        out_shape=(shaped((heads, suf, lanes), BF16),) * 2,
        in_specs=[VMEM] * 5,
        out_specs=(VMEM, VMEM),
        scratch_shapes=[pltpu.VMEM((heads, 2 * lanes, width), BF16)],
        name="qkv",
        cost_estimate=cost(2 * suf * width * 3 * heads * size, 0, 10_000_000),
    )(rows, w_query.T, w_key.T, w_value.T, key_scale)
    acc, peaks = pl.pallas_call(
        lambda *refs: suffix_kernel(*refs, tile=256),
        out_shape=(shaped((heads, suf, lanes), F32), shaped((suf, lanes), F32)),
        in_specs=[SMEM, SMEM, VMEM, VMEM],
        out_specs=(VMEM, VMEM),
        name="suffix",
        cost_estimate=cost(4 * suf * suf * heads * lanes, suf * suf * heads, 10_000_000),
    )(lengths, flag, q, kv)
    table = jnp.asarray(np.concatenate([place_table(half) for half in HALVES]))
    place = lax.axis_index("req").astype(jnp.int32).reshape(1)
    prefix_rows = owners.shape[1] * slot_rows
    prefix = pl.pallas_call(
        select_kernel,
        out_shape=shaped((heads, prefix_rows, lanes), BF16),
        in_specs=[SMEM] * 4 + [ANY] * 10,
        out_specs=VMEM,
        scratch_shapes=[pltpu.SemaphoreType.DMA((2 * owners.shape[1],))],
        name="select",
        cost_estimate=cost(0, 0, 3_000_000),
    )(membership, place, owners, table, *pools[0], *pools[1])
    part = width // 4
    rank = lax.axis_index("tp").astype(jnp.int32).reshape(1)
    chunk = suf // CHUNKS
    attended = []
    for c in range(CHUNKS):
        attended.append(
            pl.pallas_call(
                lambda *refs: attend_kernel(*refs, tile=256),
                grid=(1,),
                out_shape=shaped((chunk, heads * size), BF16),
                in_specs=[
                    SMEM,
                    pl.BlockSpec((heads, chunk, lanes), lambda i, c=c: (0, c, 0)),
                    pl.BlockSpec((heads, chunk, lanes), lambda i, c=c: (0, c, 0)),
                    pl.BlockSpec((chunk, lanes), lambda i, c=c: (c, 0)),
                    VMEM,
                ],
                out_specs=pl.BlockSpec((chunk, heads * size), lambda i: (0, 0)),
                scratch_shapes=[pltpu.VMEM((heads, chunk, lanes), F32)],
                name="attend",
                cost_estimate=cost(4 * chunk * prefix_rows * heads * lanes, chunk * prefix_rows * heads, 8_000_000),
            )(flag, q, acc, peaks, prefix)
        )
    out = None
    for c in range(CHUNKS):
        far = across(attended[c], 2)
        core = across(attended[c], 1)
        both = across(far, 1)
        operands = [lengths, rank, attended[c], core, far, both, w_out, w_core, w_far, w_both, rows, step_rates.reshape(1, width)]
        specs = [SMEM] * 2 + [VMEM] * 8 + [pl.BlockSpec((chunk, width), lambda i, c=c: (c, 0)), VMEM]
        aliases = {}
        if out is not None:
            aliases = {len(operands): 0}
            operands.append(out)
            specs.append(ANY)
        out = pl.pallas_call(
            lambda *refs, c=c: output_kernel(*refs, tile=128, start=c * chunk),
            grid=(1,),
            out_shape=shaped((part, suf), BF16),
            in_specs=specs,
            out_specs=pl.BlockSpec((part, chunk), lambda i, c=c: (0, c)),
            input_output_aliases=aliases,
            name="output",
            cost_estimate=cost(2 * chunk * width * width, 0, 6_000_000),
        )(*operands)
    return out.T.reshape(1, suf, part)


def solution(mesh):
    in_specs = (
        P("req", None, None),
        P("req"),
        P("req"),
        P(),
        P("req", "tp", None),
        P(None, "tp"),
        P(None, "tp"),
        P(None, "tp"),
        P("tp", None),
        P("tp", None),
        P(),
    )
    out_specs = P("req", None, "tp")
    return jax.shard_map(local, mesh=mesh, in_specs=in_specs, out_specs=out_specs, check_vma=False)
```

```python
import math

import jax
import jax.numpy as jnp
import numpy as np
from jax import lax
from jax.experimental import pallas as pl
from jax.experimental.pallas import tpu as pltpu
from jax.sharding import PartitionSpec as P

F32 = jnp.float32
BF16 = jnp.bfloat16
LOG2E = math.log2(math.e)
EPS = 1e-06

NX, NZ, NY = 2, 8, 4


def add3(a, b):
    return ((a[0] + b[0]) % NX, (a[1] + b[1]) % NZ, (a[2] + b[2]) % NY)


def flat3(a):
    return a[0] * NZ * NY + a[1] * NY + a[2]


def unflat3(i):
    return (i // (NZ * NY), (i // NY) % NZ, i % NY)


def fetch(array, offset):
    pairs = [(flat3(add3(unflat3(i), offset)), i) for i in range(NX * NZ * NY)]
    return lax.ppermute(array, "req", pairs)


HALVES = (
    dict(
        quad=((0, 0, 0), (0, 4, 0), (1, 0, 2), (1, 4, 2)),
        pool=((0, 0, 0), (0, 1, 0), (0, 7, 0), (0, 6, 0)),
        near=((0, 0, 1), (0, 0, 3), (1, 0, 0), (0, 0, 2)),
    ),
    dict(
        quad=((0, 0, 0), (0, 4, 0), (1, 2, 0), (1, 6, 0)),
        pool=((0, 0, 0), (0, 0, 1), (0, 0, 3), (0, 0, 2)),
        near=((0, 1, 0), (0, 7, 0), (1, 0, 0), (0, 2, 0)),
    ),
)
CHUNKS = 2
SPLIT = 3


def place_table(half):
    quads = [[add3(p, q) for q in half["quad"]] for p in half["pool"]]
    plus, minus, across, two = half["near"]
    order = [m for quad in quads for m in quad]
    order += [add3(plus, m) for quad in quads for m in quad]
    order += [add3(minus, m) for quad in quads for m in quad]
    order += [add3(across, m) for quad in quads[:SPLIT] for m in quad]
    order += [add3(two, m) for quad in quads[SPLIT:] for m in quad]
    assert sorted(flat3(m) for m in order) == list(range(64))
    table = np.zeros(64, np.int32)
    for place, m in enumerate(order):
        table[flat3(m)] = place
    return table


def dot_t(a, b):
    return lax.dot_general(a, b, (((1,), (1,)), ((), ())), preferred_element_type=F32)


def pair_lanes(scale, fill):
    return jnp.concatenate([scale, jnp.full_like(scale, fill)], axis=1)


def lane_half(lanes):
    return lax.broadcasted_iota(jnp.int32, (1, lanes), 1) < lanes // 2


def prep_kernel(block_ref, scale_ref, flag_ref, whole_ref, one_ref, two_ref):
    heads, rows, lanes = block_ref.shape
    size = lanes // 2
    first = lane_half(lanes)
    scale = scale_ref[...]
    bound = jnp.max(scale * scale) * (1.02 * LOG2E * math.sqrt(size))
    flag_ref[0] = (bound <= 60.0).astype(jnp.int32)
    for h in range(heads):
        wide = block_ref[h].astype(F32)
        mean = jnp.sum(jnp.where(first, wide * wide, 0.0), axis=-1, keepdims=True) * (1.0 / size)
        keys = wide * lax.rsqrt(mean + EPS) * pair_lanes(scale[h : h + 1], 1.0)
        block = jnp.where(first, keys, wide).astype(BF16)
        whole_ref[h] = block
        one_ref[h] = block[: rows // 2]
        two_ref[h] = block[rows // 2 :]


def qkv_kernel(hid_ref, wq_ref, wk_ref, wv_ref, scale_ref, q_ref, kv_ref, w_ref, *, tile):
    heads, suf, lanes = q_ref.shape
    size = lanes // 2
    first = lane_half(lanes)
    for h in range(heads):
        own = slice(h * size, (h + 1) * size)
        w_ref[h, :size] = wq_ref[own]
        w_ref[h, size : 2 * size] = jnp.zeros_like(wq_ref[own])
        w_ref[h, 2 * size : 3 * size] = wk_ref[own]
        w_ref[h, 3 * size :] = wv_ref[own]
    for h in range(heads):
        scale = scale_ref[h : h + 1]
        q_scale = pair_lanes(scale * (LOG2E / math.sqrt(size)), 0.0)
        k_scale = pair_lanes(scale, 1.0)
        for i in range(suf // tile):
            rows = slice(i * tile, (i + 1) * tile)
            both = dot_t(hid_ref[rows], w_ref[h])
            q, kv = both[:, :lanes], both[:, lanes:]
            q_mean = jnp.sum(q * q, axis=-1, keepdims=True) * (1.0 / size)
            k_mean = jnp.sum(jnp.where(first, kv * kv, 0.0), axis=-1, keepdims=True) * (1.0 / size)
            q_ref[h, rows] = (q * lax.rsqrt(q_mean + EPS) * q_scale).astype(BF16)
            keys = kv * lax.rsqrt(k_mean + EPS) * k_scale
            kv_ref[h, rows] = jnp.where(first, keys, kv).astype(BF16)


def suffix_kernel(len_ref, flag_ref, q_ref, kv_ref, acc_ref, peak_ref, *, tile):
    heads, suf, lanes = q_ref.shape
    first = lane_half(lanes)
    length = len_ref[0]
    safe = flag_ref[0] == 1

    @pl.when(safe)
    def _():
        qpos = lax.broadcasted_iota(jnp.int32, (tile, tile), 0)
        kpos = lax.broadcasted_iota(jnp.int32, (tile, tile), 1)
        masks = []
        for j in range(suf // tile):
            inside = kpos + j * tile < length
            masks.append((inside & (kpos <= qpos), inside))
        for h in range(heads):
            for i in range(suf // tile):
                rows = slice(i * tile, (i + 1) * tile)
                total = None
                for j in range(i + 1):
                    keys = kv_ref[h, j * tile : (j + 1) * tile]
                    weights = jnp.exp2(dot_t(q_ref[h, rows], keys))
                    weights = jnp.where(masks[j][0 if i == j else 1], weights, 0.0).astype(BF16)
                    ones_values = jnp.where(first, jnp.ones_like(keys), keys)
                    part = jnp.dot(weights, ones_values, preferred_element_type=F32)
                    total = part if total is None else total + part
                acc_ref[h, rows] = total

    @pl.when(jnp.logical_not(safe))
    def _():
        lane = lax.broadcasted_iota(jnp.int32, (1, lanes), 1)
        peak_ref[...] = jnp.zeros_like(peak_ref)

        def head(h, carry):
            for i in range(suf // tile):
                rows = slice(i * tile, (i + 1) * tile)
                count = (i + 1) * tile
                qpos = lax.broadcasted_iota(jnp.int32, (tile, count), 0) + i * tile
                kpos = lax.broadcasted_iota(jnp.int32, (tile, count), 1)
                keys = kv_ref[h, :count]
                scores = jnp.where(
                    (kpos <= qpos) & (kpos < length), dot_t(q_ref[h, rows], keys), -1e30
                )
                peak = jnp.max(scores, axis=-1, keepdims=True)
                weights = jnp.exp2(scores - peak).astype(BF16)
                ones_values = jnp.where(first, jnp.ones_like(keys), keys)
                acc_ref[h, rows] = jnp.dot(weights, ones_values, preferred_element_type=F32)
                peak_ref[rows] = jnp.where(lane == h, peak, peak_ref[rows])
            return carry

        lax.fori_loop(0, heads, head, 0)


def pack_kernel(*refs):
    quads, outs, sems = refs[:8], refs[8:12], refs[12]
    copies = []
    for half in range(2):
        pool, head = outs[2 * half : 2 * half + 2]
        for n in range(4):
            quad = quads[4 * half + n]
            copies.append((quad, pool.at[pl.ds(4 * n, 4)]))
            if n < SPLIT:
                copies.append((quad, head.at[pl.ds(4 * n, 4)]))
    started = [pltpu.make_async_copy(a, b, sems.at[i]) for i, (a, b) in enumerate(copies)]
    for copy in started:
        copy.start()
    for copy in started:
        copy.wait()


def select_kernel(member_ref, place_ref, owners_ref, table_ref, *rest):
    blocks = (rest[:5], rest[5:10])
    kv_ref, sems = rest[10:]
    group = member_ref[0]
    me = place_ref[0]
    slots = owners_ref.shape[1]
    part = kv_ref.shape[1] // (2 * slots)
    bounds = (0, 16, 32, 48, 48 + 4 * SPLIT, 64)

    def start(j, carry):
        owner = owners_ref[group, j]
        rel = (
            ((owner ^ me) & 32)
            + ((((owner >> 2) - (me >> 2)) & 7) << 2)
            + ((owner - me) & 3)
        )
        for half in range(2):
            place = table_ref[half * 64 + rel]
            row = pl.multiple_of((2 * j + half) * part, part)
            goal = kv_ref.at[:, pl.ds(row, part), :]
            for n, ref in enumerate(blocks[half]):
                low, high = bounds[n], bounds[n + 1]

                @pl.when((place >= low) & (place < high))
                def _(ref=ref, low=low):
                    pltpu.make_async_copy(ref.at[place - low], goal, sems.at[2 * j + half]).start()

        return carry

    lax.fori_loop(0, slots, start, 0)

    def finish(j, carry):
        row = pl.multiple_of(j * part, part)
        goal = kv_ref.at[:, pl.ds(row, part), :]
        pltpu.make_async_copy(blocks[0][0].at[0], goal, sems.at[j]).wait()
        return carry

    lax.fori_loop(0, 2 * slots, finish, 0)


def attend_kernel(flag_ref, q_ref, acc_ref, peak_ref, kv_ref, out_ref, total_ref, *, tile):
    heads, rows, lanes = q_ref.shape
    size = lanes // 2
    count = kv_ref.shape[1]
    first = lane_half(lanes)
    safe = flag_ref[0] == 1

    @pl.when(safe)
    def _():
        for h in range(heads):
            total = acc_ref[h]
            for j in range(count // tile):
                keys = kv_ref[h, j * tile : (j + 1) * tile]
                weights = jnp.exp2(dot_t(q_ref[h], keys)).astype(BF16)
                ones_values = jnp.where(first, jnp.ones_like(keys), keys)
                total = total + jnp.dot(weights, ones_values, preferred_element_type=F32)
            total_ref[h] = total

    @pl.when(jnp.logical_not(safe))
    def _():
        lane = lax.broadcasted_iota(jnp.int32, (1, lanes), 1)

        def head(h, carry):
            keys = kv_ref[h]
            scores = dot_t(q_ref[h], keys)
            near = jnp.max(jnp.where(lane == h, peak_ref[...], -3e38), axis=-1, keepdims=True)
            peak = jnp.maximum(jnp.max(scores, axis=-1, keepdims=True), near)
            weights = jnp.exp2(scores - peak).astype(BF16)
            ones_values = jnp.where(first, jnp.ones_like(keys), keys)
            total = jnp.dot(weights, ones_values, preferred_element_type=F32)
            total_ref[h] = total + acc_ref[h] * jnp.exp2(near - peak)
            return carry

        lax.fori_loop(0, heads, head, 0)

    for h in range(heads):
        total = total_ref[h]
        value = total / pltpu.roll(total, size, 1)
        out_ref[:, h * size : (h + 1) * size] = value[:, size:].astype(BF16)


def output_kernel(
    len_ref, rank_ref, a0, a1, a2, a3, w0, w1, w2, w3, hid_ref, rate_ref, *rest, tile, start
):
    out_ref, moved_ref = rest[-2:]
    count, width = hid_ref.shape
    part = out_ref.shape[0]
    length = len_ref[0]
    rank = rank_ref[0]
    cols = [slice(n * tile, (n + 1) * tile) for n in range(width // tile)]
    square = None
    for col in cols:
        branch = jnp.dot(a0[...], w0[:, col], preferred_element_type=F32)
        for a, w in ((a1, w1), (a2, w2), (a3, w3)):
            branch += jnp.dot(a[...], w[:, col], preferred_element_type=F32)
        moved_ref[:, col] = branch
        part_square = jnp.sum(branch * branch, axis=-1, keepdims=True)
        square = part_square if square is None else square + part_square
    gain = lax.rsqrt(square * (1.0 / width) + EPS)
    square = None
    for col in cols:
        state = hid_ref[:, col].astype(F32)
        moved = state + rate_ref[:, col] * (moved_ref[:, col] * gain - state)
        moved_ref[:, col] = moved
        part_square = jnp.sum(moved * moved, axis=-1, keepdims=True)
        square = part_square if square is None else square + part_square
    norm = lax.rsqrt(square * (1.0 / width) + EPS)
    pos = lax.broadcasted_iota(jnp.int32, (count, 1), 0) + start
    for t in range(width // part):

        @pl.when(rank == t)
        def _(t=t):
            mine = moved_ref[:, t * part : (t + 1) * part]
            out_ref[...] = jnp.where(pos < length, mine * norm, 0.0).T.astype(BF16)


VMEM = pl.BlockSpec(memory_space=pltpu.VMEM)
SMEM = pl.BlockSpec(memory_space=pltpu.SMEM)
ANY = pl.BlockSpec(memory_space=pl.ANY)


def across(array, bit):
    return lax.ppermute(array, "tp", [(i, i ^ bit) for i in range(4)])


def shaped(shape, dtype):
    return jax.ShapeDtypeStruct(shape, dtype)


def vmem(mebibytes):
    return pltpu.CompilerParams(vmem_limit_bytes=mebibytes << 20)


def cost(flops, exps, moved):
    return pl.CostEstimate(flops=flops, transcendentals=exps, bytes_accessed=moved)


def gather_pools(whole, halves):
    far = fetch(whole, (0, 4, 0))
    part = whole.shape[1] // 2
    quads = []
    for n, (half, mine) in enumerate(zip(HALVES, halves)):
        pair = jnp.stack([mine, far[:, n * part : (n + 1) * part]])
        quads.append(jnp.concatenate([pair, fetch(pair, half["quad"][2])]))
    held = [
        [quad] + [fetch(quad, offset) for offset in half["pool"][1:]]
        for quad, half in zip(quads, HALVES)
    ]
    shape = quads[0].shape[1:]
    packed = pl.pallas_call(
        pack_kernel,
        out_shape=(shaped((16,) + shape, BF16), shaped((4 * SPLIT,) + shape, BF16)) * 2,
        in_specs=[ANY] * 8,
        out_specs=(ANY,) * 4,
        scratch_shapes=[pltpu.SemaphoreType.DMA((2 * (4 + SPLIT),))],
        name="pack",
        compiler_params=vmem(1),
        cost_estimate=cost(0, 0, 4_000_000),
    )(*held[0], *held[1])
    result = []
    for n, half in enumerate(HALVES):
        plus, minus, across_x, two = half["near"]
        pool, head = packed[2 * n : 2 * n + 2]
        result.append(
            (pool, fetch(pool, plus), fetch(pool, minus), fetch(head, across_x), fetch(held[n][3], two))
        )
    return result, quads


def local(
    hidden,
    membership,
    lengths,
    owners,
    prefix_cache,
    w_query,
    w_key,
    w_value,
    key_scale,
    w_out,
    step_rates,
):
    _, suf, width = hidden.shape
    heads, size = key_scale.shape
    lanes = 2 * size
    slot_rows = prefix_cache.shape[0]
    rows = hidden.reshape(suf, width)
    block = (heads, slot_rows, lanes)
    half_block = (heads, slot_rows // 2, lanes)
    flag, whole, one, two = pl.pallas_call(
        prep_kernel,
        out_shape=(
            shaped((1,), jnp.int32), shaped(block, BF16), shaped(half_block, BF16), shaped(half_block, BF16),
        ),
        in_specs=[VMEM, VMEM],
        out_specs=(SMEM, VMEM, VMEM, VMEM),
        name="prep",
        compiler_params=vmem(2),
        cost_estimate=cost(0, 0, 300_000),
    )(jnp.transpose(prefix_cache, (1, 0, 2)), key_scale)
    pools, quads = gather_pools(whole, (one, two))
    w_late = lax.optimization_barrier((w_out, *quads))[0]
    w_far = across(w_late, 2)
    q, kv = pl.pallas_call(
        lambda *refs: qkv_kernel(*refs, tile=256),
        out_shape=(shaped((heads, suf, lanes), BF16),) * 2,
        in_specs=[VMEM] * 5,
        out_specs=(VMEM, VMEM),
        scratch_shapes=[pltpu.VMEM((heads, 2 * lanes, width), BF16)],
        name="qkv",
        compiler_params=vmem(14),
        cost_estimate=cost(2 * suf * width * 3 * heads * size, 0, 10_000_000),
    )(rows, w_query.T, w_key.T, w_value.T, key_scale)
    acc, peaks = pl.pallas_call(
        lambda *refs: suffix_kernel(*refs, tile=256),
        out_shape=(shaped((heads, suf, lanes), F32), shaped((suf, lanes), F32)),
        in_specs=[SMEM, SMEM, VMEM, VMEM],
        out_specs=(VMEM, VMEM),
        name="suffix",
        compiler_params=vmem(10),
        cost_estimate=cost(4 * suf * suf * heads * lanes, suf * suf * heads, 10_000_000),
    )(lengths, flag, q, kv)
    w_late, far_late = lax.optimization_barrier((w_out, w_far, peaks))[:2]
    w_core = across(w_late, 1)
    w_both = across(far_late, 1)
    table = jnp.asarray(np.concatenate([place_table(half) for half in HALVES]))
    place = lax.axis_index("req").astype(jnp.int32).reshape(1)
    prefix_rows = owners.shape[1] * slot_rows
    prefix = pl.pallas_call(
        select_kernel,
        out_shape=shaped((heads, prefix_rows, lanes), BF16),
        in_specs=[SMEM] * 4 + [ANY] * 10,
        out_specs=VMEM,
        scratch_shapes=[pltpu.SemaphoreType.DMA((2 * owners.shape[1],))],
        name="select",
        compiler_params=vmem(4),
        cost_estimate=cost(0, 0, 3_000_000),
    )(membership, place, owners, table, *pools[0], *pools[1])
    part = width // 4
    rank = lax.axis_index("tp").astype(jnp.int32).reshape(1)
    chunk = suf // CHUNKS
    attended = []
    for c in range(CHUNKS):
        attended.append(
            pl.pallas_call(
                lambda *refs: attend_kernel(*refs, tile=256),
                grid=(1,),
                out_shape=shaped((chunk, heads * size), BF16),
                in_specs=[
                    SMEM,
                    pl.BlockSpec((heads, chunk, lanes), lambda i, c=c: (0, c, 0)),
                    pl.BlockSpec((heads, chunk, lanes), lambda i, c=c: (0, c, 0)),
                    pl.BlockSpec((chunk, lanes), lambda i, c=c: (c, 0)),
                    VMEM,
                ],
                out_specs=pl.BlockSpec((chunk, heads * size), lambda i: (0, 0)),
                scratch_shapes=[pltpu.VMEM((heads, chunk, lanes), F32)],
                name="attend",
        compiler_params=vmem(14),
                cost_estimate=cost(4 * chunk * prefix_rows * heads * lanes, chunk * prefix_rows * heads, 8_000_000),
            )(flag, q, acc, peaks, prefix)
        )
    out = None
    for c in range(CHUNKS):
        far = across(attended[c], 2)
        core = across(attended[c], 1)
        both = across(attended[c], 3)
        operands = [lengths, rank, attended[c], core, far, both, w_out, w_core, w_far, w_both, rows, step_rates.reshape(1, width)]
        specs = [SMEM] * 2 + [VMEM] * 8 + [pl.BlockSpec((chunk, width), lambda i, c=c: (c, 0)), VMEM]
        aliases = {}
        if out is not None:
            aliases = {len(operands): 0}
            operands.append(out)
            specs.append(ANY)
        out = pl.pallas_call(
            lambda *refs, c=c: output_kernel(*refs, tile=256, start=c * chunk),
            grid=(1,),
            out_shape=shaped((part, suf), BF16),
            in_specs=specs,
            out_specs=pl.BlockSpec((part, chunk), lambda i, c=c: (0, c)),
            input_output_aliases=aliases,
            scratch_shapes=[pltpu.VMEM((chunk, width), F32)],
            name="output",
        compiler_params=vmem(20),
            cost_estimate=cost(2 * chunk * width * width, 0, 6_000_000),
        )(*operands)
    return out.T.reshape(1, suf, part)


def solution(mesh):
    in_specs = (
        P("req", None, None),
        P("req"),
        P("req"),
        P(),
        P("req", "tp", None),
        P(None, "tp"),
        P(None, "tp"),
        P(None, "tp"),
        P("tp", None),
        P("tp", None),
        P(),
    )
    out_specs = P("req", None, "tp")
    return jax.shard_map(local, mesh=mesh, in_specs=in_specs, out_specs=out_specs, check_vma=False)
```

```python
import math

import jax
import jax.numpy as jnp
import numpy as np
from jax import lax
from jax.experimental import pallas as pl
from jax.experimental.pallas import tpu as pltpu
from jax.sharding import PartitionSpec as P


F32 = jnp.float32
BF16 = jnp.bfloat16
LOG2E = math.log2(math.e)
EPS = 1e-06

NX, NZ, NY = 2, 8, 4


def add3(a, b):
    return ((a[0] + b[0]) % NX, (a[1] + b[1]) % NZ, (a[2] + b[2]) % NY)


def flat3(a):
    return a[0] * NZ * NY + a[1] * NY + a[2]


def unflat3(i):
    return (i // (NZ * NY), (i // NY) % NZ, i % NY)


def fetch(array, offset):
    pairs = [(flat3(add3(unflat3(i), offset)), i) for i in range(NX * NZ * NY)]
    return lax.ppermute(array, "req", pairs)


QUAD = ((0, 0, 0), (1, 0, 0), (0, 4, 0), (1, 4, 0))
HALVES = (
    dict(
        pool=((0, 0, 0), (0, 1, 0), (0, 7, 0), (0, 6, 0)),
        near=((0, 0, 1), (0, 0, 3), (0, 0, 2)),
        sends=((0, 0, 1), (0, 0, 3), (0, 0, 2)),
    ),
    dict(
        pool=((0, 0, 0), (0, 0, 1), (0, 0, 3), (0, 0, 2)),
        near=((0, 1, 0), (0, 7, 0), (0, 2, 0)),
        sends=((0, 1, 0), (0, 7, 0), (0, 2, 0), (0, 6, 0)),
    ),
)
CAP = 8
CHUNKS = 2


def minus3(a):
    return (-a[0] % NX, -a[1] % NZ, -a[2] % NY)


def place_table(half):
    pool = [add3(p, q) for p in half["pool"] for q in QUAD]
    order = [add3(n, m) for n in ((0, 0, 0),) + half["near"] for m in pool]
    assert sorted(flat3(m) for m in order) == list(range(64))
    table = np.zeros(64, np.int32)
    for place, m in enumerate(order):
        table[flat3(m)] = place
    return table


def member_spot(target):
    for n, half in enumerate(HALVES):
        for k, p in enumerate(half["pool"]):
            for b, q in enumerate(QUAD):
                if add3(p, q) == target:
                    return n, k, b
    raise ValueError(target)


def dot_t(a, b):
    return lax.dot_general(a, b, (((1,), (1,)), ((), ())), preferred_element_type=F32)


def pair_lanes(scale, fill):
    return jnp.concatenate([scale, jnp.full_like(scale, fill)], axis=1)


def lane_half(lanes):
    return lax.broadcasted_iota(jnp.int32, (1, lanes), 1) < lanes // 2


def prep_kernel(member_ref, block_ref, scale_ref, flag_ref, whole_ref):
    heads, rows, lanes = block_ref.shape
    size = lanes // 2
    first = lane_half(lanes)
    scale = scale_ref[...]
    bound = jnp.max(scale * scale) * (1.02 * LOG2E * math.sqrt(size))
    flag_ref[0] = (bound <= 60.0).astype(jnp.int32)
    for h in range(heads):
        wide = block_ref[h].astype(F32)
        mean = jnp.sum(jnp.where(first, wide * wide, 0.0), axis=-1, keepdims=True) * (1.0 / size)
        keys = wide * lax.rsqrt(mean + EPS) * pair_lanes(scale[h : h + 1], 1.0)
        whole_ref[h] = jnp.where(first, keys, wide).astype(BF16)
    whole_ref[heads] = jnp.full((rows, lanes), member_ref[0].astype(F32)).astype(BF16)


def qkv_kernel(hid_ref, wq_ref, wk_ref, wv_ref, scale_ref, q_ref, kv_ref, w_ref, *, tile):
    heads, suf, lanes = q_ref.shape
    size = lanes // 2
    first = lane_half(lanes)
    for h in range(heads):
        own = slice(h * size, (h + 1) * size)
        w_ref[h, :size] = wq_ref[own]
        w_ref[h, size : 2 * size] = jnp.zeros_like(wq_ref[own])
        w_ref[h, 2 * size : 3 * size] = wk_ref[own]
        w_ref[h, 3 * size :] = wv_ref[own]
    for h in range(heads):
        scale = scale_ref[h : h + 1]
        q_scale = pair_lanes(scale * (LOG2E / math.sqrt(size)), 0.0)
        k_scale = pair_lanes(scale, 1.0)
        for i in range(suf // tile):
            rows = slice(i * tile, (i + 1) * tile)
            both = dot_t(hid_ref[rows], w_ref[h])
            q, kv = both[:, :lanes], both[:, lanes:]
            q_mean = jnp.sum(q * q, axis=-1, keepdims=True) * (1.0 / size)
            k_mean = jnp.sum(jnp.where(first, kv * kv, 0.0), axis=-1, keepdims=True) * (1.0 / size)
            q_ref[h, rows] = (q * lax.rsqrt(q_mean + EPS) * q_scale).astype(BF16)
            keys = kv * lax.rsqrt(k_mean + EPS) * k_scale
            kv_ref[h, rows] = jnp.where(first, keys, kv).astype(BF16)


def suffix_kernel(len_ref, flag_ref, q_ref, kv_ref, acc_ref, peak_ref, *, tile):
    heads, suf, lanes = q_ref.shape
    first = lane_half(lanes)
    length = len_ref[0]
    safe = flag_ref[0] == 1

    @pl.when(safe)
    def _():
        qpos = lax.broadcasted_iota(jnp.int32, (tile, tile), 0)
        kpos = lax.broadcasted_iota(jnp.int32, (tile, tile), 1)
        masks = []
        for j in range(suf // tile):
            inside = kpos + j * tile < length
            masks.append((inside & (kpos <= qpos), inside))
        for h in range(heads):
            for i in range(suf // tile):
                rows = slice(i * tile, (i + 1) * tile)
                total = None
                for j in range(i + 1):
                    keys = kv_ref[h, j * tile : (j + 1) * tile]
                    weights = jnp.exp2(dot_t(q_ref[h, rows], keys))
                    weights = jnp.where(masks[j][0 if i == j else 1], weights, 0.0).astype(BF16)
                    ones_values = jnp.where(first, jnp.ones_like(keys), keys)
                    part = jnp.dot(weights, ones_values, preferred_element_type=F32)
                    total = part if total is None else total + part
                acc_ref[h, rows] = total

    @pl.when(jnp.logical_not(safe))
    def _():
        lane = lax.broadcasted_iota(jnp.int32, (1, lanes), 1)
        peak_ref[...] = jnp.zeros_like(peak_ref)

        def head(h, carry):
            for i in range(suf // tile):
                rows = slice(i * tile, (i + 1) * tile)
                count = (i + 1) * tile
                qpos = lax.broadcasted_iota(jnp.int32, (tile, count), 0) + i * tile
                kpos = lax.broadcasted_iota(jnp.int32, (tile, count), 1)
                keys = kv_ref[h, :count]
                scores = jnp.where(
                    (kpos <= qpos) & (kpos < length), dot_t(q_ref[h, rows], keys), -1e30
                )
                peak = jnp.max(scores, axis=-1, keepdims=True)
                weights = jnp.exp2(scores - peak).astype(BF16)
                ones_values = jnp.where(first, jnp.ones_like(keys), keys)
                acc_ref[h, rows] = jnp.dot(weights, ones_values, preferred_element_type=F32)
                peak_ref[rows] = jnp.where(lane == h, peak, peak_ref[rows])
            return carry

        lax.fori_loop(0, heads, head, 0)


def split_kernel(a_ref, b_ref, c_ref, d_ref, one_ref, two_ref):
    rows = one_ref.shape[2]
    for n, ref in enumerate((a_ref, b_ref, c_ref, d_ref)):
        one_ref[n] = ref[:, :rows]
        two_ref[n] = ref[:, rows:]


def plan_kernel(member_ref, place_ref, owners_ref, table_ref, send_ref, recv_ref, over_ref, count_ref):
    group = member_ref[0]
    me = place_ref[0]
    groups, slots = owners_ref.shape

    def spots(owner):
        rel = (
            ((owner ^ me) & 32)
            + ((((owner >> 2) - (me >> 2)) & 7) << 2)
            + ((owner - me) & 3)
        )
        return table_ref[rel], table_ref[64 + rel]

    def by_group(g, most):
        for n in range(8):
            count_ref[n] = 0

        def by_slot(j, carry):
            most, held = carry
            owner = owners_ref[g, j]
            after = []
            for half, (spot, color) in enumerate(zip(spots(owner), (owner & 3, (owner >> 2) & 3))):
                send_ref[half * 64 + g * slots + held[half]] = spot
                after.append(held[half] + (spot < 16).astype(jnp.int32))
                seen = count_ref[half * 4 + color] + 1
                count_ref[half * 4 + color] = seen
                most = jnp.maximum(most, seen)
            return most, tuple(after)

        return lax.fori_loop(0, slots, by_slot, (most, (jnp.int32(0), jnp.int32(0))))[0]

    most = lax.fori_loop(0, groups, by_group, jnp.int32(0))
    over_ref[0] = (most > CAP).astype(jnp.int32)
    for n in range(8):
        count_ref[n] = 0

    def by_own(j, carry):
        for half, spot in enumerate(spots(owners_ref[group, j])):
            source = spot >> 4
            rank = count_ref[half * 4 + source]
            count_ref[half * 4 + source] = rank + 1
            recv_ref[half * slots + j] = source * 16 + rank
        return carry

    lax.fori_loop(0, slots, by_own, 0)


def pack_kernel(member_ref, send_ref, *rest, start):
    quads, outs, pool_ref = (rest[:4], rest[4:8]), rest[8:-1], rest[-1]
    heads = pool_ref.shape[2]
    for half in range(2):
        for n in range(4):
            pool_ref[half, 4 * n : 4 * n + 4] = quads[half][n][:, :heads]

    def wanted(target):
        n, k, b = member_spot(target)
        value = quads[n][k][b, heads].astype(F32)
        return jnp.max(value).astype(jnp.int32)

    jobs = []
    place = 0
    for n, half in enumerate(HALVES):
        if start == 0:
            jobs.append((outs[place], n, member_ref[0], 0))
            place += 1
        for k, offset in enumerate(half["sends"]):
            out = outs[place]
            place += 1
            jobs.append((out, n, wanted(minus3(offset)), start + (out.shape[0] if k == 3 else 0)))
    for out, half, group, first in jobs:

        def copy(i, carry, out=out, half=half, group=group, first=first):
            spot = send_ref[half * 64 + group * 16 + first + i] & 15
            out[i] = pool_ref[half, spot]
            return carry

        lax.fori_loop(0, out.shape[0], copy, 0)


def select_kernel(recv_ref, *rest):
    kv_ref, sems = rest[-2:]
    blocks = rest[:-2]
    slots = recv_ref.shape[0] // 2
    part = kv_ref.shape[1] // (2 * slots)
    spots = []
    for start in range(0, CAP * (2 if len(blocks) > 9 else 1), CAP):
        for n, half in enumerate(HALVES):
            if start == 0:
                spots.append((n, 0, 0))
            for k in range(len(half["sends"])):
                spots.append((n, min(k, 2) + 1, start + (CAP // 2 if k == 3 else 0)))
    assert len(spots) == len(blocks)

    def begin(j, carry):
        for half in range(2):
            code = recv_ref[half * slots + j]
            row = pl.multiple_of((2 * j + half) * part, part)
            goal = kv_ref.at[:, pl.ds(row, part), :]
            for ref, (n, source, low) in zip(blocks, spots):
                if n != half:
                    continue
                least = source * 16 + low

                @pl.when((code >= least) & (code < least + ref.shape[0]))
                def _(ref=ref, least=least):
                    pltpu.make_async_copy(ref.at[code - least], goal, sems.at[2 * j + half]).start()

        return carry

    lax.fori_loop(0, slots, begin, 0)

    def finish(j, carry):
        row = pl.multiple_of(j * part, part)
        goal = kv_ref.at[:, pl.ds(row, part), :]
        pltpu.make_async_copy(blocks[0].at[0], goal, sems.at[j]).wait()
        return carry

    lax.fori_loop(0, 2 * slots, finish, 0)


def attend_kernel(flag_ref, q_ref, acc_ref, peak_ref, kv_ref, out_ref, total_ref, *, tile):
    heads, _, lanes = q_ref.shape
    size = lanes // 2
    count = kv_ref.shape[1]
    first = lane_half(lanes)
    safe = flag_ref[0] == 1

    @pl.when(safe)
    def _():
        for h in range(heads):
            total = acc_ref[h]
            for j in range(count // tile):
                keys = kv_ref[h, j * tile : (j + 1) * tile]
                weights = jnp.exp2(dot_t(q_ref[h], keys)).astype(BF16)
                ones_values = jnp.where(first, jnp.ones_like(keys), keys)
                total = total + jnp.dot(weights, ones_values, preferred_element_type=F32)
            total_ref[h] = total

    @pl.when(jnp.logical_not(safe))
    def _():
        lane = lax.broadcasted_iota(jnp.int32, (1, lanes), 1)

        def head(h, carry):
            keys = kv_ref[h]
            scores = dot_t(q_ref[h], keys)
            near = jnp.max(jnp.where(lane == h, peak_ref[...], -3e38), axis=-1, keepdims=True)
            peak = jnp.maximum(jnp.max(scores, axis=-1, keepdims=True), near)
            weights = jnp.exp2(scores - peak).astype(BF16)
            ones_values = jnp.where(first, jnp.ones_like(keys), keys)
            total = jnp.dot(weights, ones_values, preferred_element_type=F32)
            total_ref[h] = total + acc_ref[h] * jnp.exp2(near - peak)
            return carry

        lax.fori_loop(0, heads, head, 0)

    for h in range(heads):
        total = total_ref[h]
        value = total / pltpu.roll(total, size, 1)
        out_ref[:, h * size : (h + 1) * size] = value[:, size:].astype(BF16)


def output_kernel(
    len_ref, rank_ref, a0, a1, a2, a3, w0, w1, w2, w3, hid_ref, rate_ref, *rest, tile, start
):
    out_ref, moved_ref = rest[-2:]
    count, width = hid_ref.shape
    part = out_ref.shape[0]
    length = len_ref[0]
    rank = rank_ref[0]
    cols = [slice(n * tile, (n + 1) * tile) for n in range(width // tile)]
    square = None
    for col in cols:
        branch = jnp.dot(a0[...], w0[:, col], preferred_element_type=F32)
        for a, w in ((a1, w1), (a2, w2), (a3, w3)):
            branch += jnp.dot(a[...], w[:, col], preferred_element_type=F32)
        moved_ref[:, col] = branch
        part_square = jnp.sum(branch * branch, axis=-1, keepdims=True)
        square = part_square if square is None else square + part_square
    gain = lax.rsqrt(square * (1.0 / width) + EPS)
    square = None
    for col in cols:
        state = hid_ref[:, col].astype(F32)
        moved = state + rate_ref[:, col] * (moved_ref[:, col] * gain - state)
        moved_ref[:, col] = moved
        part_square = jnp.sum(moved * moved, axis=-1, keepdims=True)
        square = part_square if square is None else square + part_square
    norm = lax.rsqrt(square * (1.0 / width) + EPS)
    pos = lax.broadcasted_iota(jnp.int32, (count, 1), 0) + start
    for t in range(width // part):

        @pl.when(rank == t)
        def _(t=t):
            mine = moved_ref[:, t * part : (t + 1) * part]
            out_ref[...] = jnp.where(pos < length, mine * norm, 0.0).T.astype(BF16)


VMEM = pl.BlockSpec(memory_space=pltpu.VMEM)
SMEM = pl.BlockSpec(memory_space=pltpu.SMEM)
ANY = pl.BlockSpec(memory_space=pl.ANY)


def across(array, bit):
    return lax.ppermute(array, "tp", [(i, i ^ bit) for i in range(4)])


def shaped(shape, dtype):
    return jax.ShapeDtypeStruct(shape, dtype)


def vmem(mebibytes):
    return pltpu.CompilerParams(vmem_limit_bytes=mebibytes << 20)


def cost(flops, exps, moved):
    return pl.CostEstimate(flops=flops, transcendentals=exps, bytes_accessed=moved)


def gather_prefix(whole, membership, owners):
    planes, rows, lanes = whole.shape
    heads, part, slots = planes - 1, rows // 2, owners.shape[1]
    place = lax.axis_index("req").astype(jnp.int32).reshape(1)
    table = jnp.asarray(np.concatenate([place_table(half) for half in HALVES]))
    send, recv, over = pl.pallas_call(
        plan_kernel,
        out_shape=(shaped((128,), jnp.int32), shaped((2 * slots,), jnp.int32), shaped((1,), jnp.int32)),
        in_specs=[SMEM] * 4,
        out_specs=(SMEM,) * 3,
        scratch_shapes=[pltpu.SMEM((8,), jnp.int32)],
        name="plan",
        compiler_params=vmem(1),
        cost_estimate=cost(0, 0, 1_000_000),
    )(membership, place, owners, table)
    quads = pl.pallas_call(
        split_kernel,
        out_shape=(shaped((4, planes, part, lanes), BF16),) * 2,
        in_specs=[VMEM] * 4,
        out_specs=(VMEM, VMEM),
        name="split",
        compiler_params=vmem(2),
        cost_estimate=cost(0, 0, 600_000),
    )(whole, *[fetch(whole, offset) for offset in QUAD[1:]])
    held = []
    for quad, half in zip(quads, HALVES):
        held += [quad] + [fetch(quad, offset) for offset in half["pool"][1:]]

    def one_round(start):
        shapes, offsets = [], []
        for half in HALVES:
            if start == 0:
                shapes.append(16)
                offsets.append(None)
            for offset in half["sends"]:
                shapes.append(CAP // 2 if len(half["sends"]) == 4 and offset[1] in (2, 6) else CAP)
                offsets.append(offset)
        packed = pl.pallas_call(
            lambda *refs: pack_kernel(*refs, start=start),
            out_shape=tuple(shaped((n, heads, part, lanes), BF16) for n in shapes),
            in_specs=[SMEM] * 2 + [VMEM] * 8,
            out_specs=(VMEM,) * len(shapes),
            scratch_shapes=[pltpu.VMEM((2, 16, heads, part, lanes), BF16)],
            name="pack",
            compiler_params=vmem(8),
            cost_estimate=cost(0, 0, 4_000_000),
        )(membership, send, *held)
        return [a if o is None else fetch(a, o) for a, o in zip(packed, offsets)]

    def select(arrays):
        return pl.pallas_call(
            select_kernel,
            out_shape=shaped((heads, slots * rows, lanes), BF16),
            in_specs=[SMEM] + [ANY] * len(arrays),
            out_specs=VMEM,
            scratch_shapes=[pltpu.SemaphoreType.DMA((2 * slots,))],
            name="select",
            compiler_params=vmem(4),
            cost_estimate=cost(0, 0, 3_000_000),
        )(recv, *arrays)

    arrays = one_round(0)
    prefix = lax.cond(
        over[0] > 0,
        lambda: select(arrays + one_round(CAP)),
        lambda: select(arrays),
    )
    return prefix


def local(
    hidden,
    membership,
    lengths,
    owners,
    prefix_cache,
    w_query,
    w_key,
    w_value,
    key_scale,
    w_out,
    step_rates,
):
    _, suf, width = hidden.shape
    heads, size = key_scale.shape
    lanes = 2 * size
    slot_rows = prefix_cache.shape[0]
    rows = hidden.reshape(suf, width)
    flag, whole = pl.pallas_call(
        prep_kernel,
        out_shape=(shaped((1,), jnp.int32), shaped((heads + 1, slot_rows, lanes), BF16)),
        in_specs=[SMEM, VMEM, VMEM],
        out_specs=(SMEM, VMEM),
        name="prep",
        compiler_params=vmem(2),
        cost_estimate=cost(0, 0, 300_000),
    )(membership, jnp.transpose(prefix_cache, (1, 0, 2)), key_scale)
    prefix = gather_prefix(whole, membership, owners)
    w_far = across(w_out, 2)
    q, kv = pl.pallas_call(
        lambda *refs: qkv_kernel(*refs, tile=256),
        out_shape=(shaped((heads, suf, lanes), BF16),) * 2,
        in_specs=[VMEM] * 5,
        out_specs=(VMEM, VMEM),
        scratch_shapes=[pltpu.VMEM((heads, 2 * lanes, width), BF16)],
        name="qkv",
        compiler_params=vmem(14),
        cost_estimate=cost(2 * suf * width * 3 * heads * size, 0, 10_000_000),
    )(rows, w_query.T, w_key.T, w_value.T, key_scale)
    acc, peaks = pl.pallas_call(
        lambda *refs: suffix_kernel(*refs, tile=256),
        out_shape=(shaped((heads, suf, lanes), F32), shaped((suf, lanes), F32)),
        in_specs=[SMEM, SMEM, VMEM, VMEM],
        out_specs=(VMEM, VMEM),
        name="suffix",
        compiler_params=vmem(10),
        cost_estimate=cost(4 * suf * suf * heads * lanes, suf * suf * heads, 10_000_000),
    )(lengths, flag, q, kv)
    w_core = across(w_out, 1)
    w_both = across(w_far, 1)
    prefix_rows = prefix.shape[1]
    part = width // 4
    rank = lax.axis_index("tp").astype(jnp.int32).reshape(1)
    chunk = suf // CHUNKS
    attended = []
    for c in range(CHUNKS):
        attended.append(
            pl.pallas_call(
                lambda *refs: attend_kernel(*refs, tile=256),
                grid=(1,),
                out_shape=shaped((chunk, heads * size), BF16),
                in_specs=[
                    SMEM,
                    pl.BlockSpec((heads, chunk, lanes), lambda i, c=c: (0, c, 0)),
                    pl.BlockSpec((heads, chunk, lanes), lambda i, c=c: (0, c, 0)),
                    pl.BlockSpec((chunk, lanes), lambda i, c=c: (c, 0)),
                    VMEM,
                ],
                out_specs=pl.BlockSpec((chunk, heads * size), lambda i: (0, 0)),
                scratch_shapes=[pltpu.VMEM((heads, chunk, lanes), F32)],
                name="attend",
        compiler_params=vmem(14),
                cost_estimate=cost(4 * chunk * prefix_rows * heads * lanes, chunk * prefix_rows * heads, 8_000_000),
            )(flag, q, acc, peaks, prefix)
        )
    out = None
    for c in range(CHUNKS):
        far = across(attended[c], 2)
        core = across(attended[c], 1)
        both = across(attended[c], 3)
        operands = [lengths, rank, attended[c], core, far, both, w_out, w_core, w_far, w_both, rows, step_rates.reshape(1, width)]
        specs = [SMEM] * 2 + [VMEM] * 8 + [pl.BlockSpec((chunk, width), lambda i, c=c: (c, 0)), VMEM]
        aliases = {}
        if out is not None:
            aliases = {len(operands): 0}
            operands.append(out)
            specs.append(ANY)
        out = pl.pallas_call(
            lambda *refs, c=c: output_kernel(*refs, tile=256, start=c * chunk),
            grid=(1,),
            out_shape=shaped((part, suf), BF16),
            in_specs=specs,
            out_specs=pl.BlockSpec((part, chunk), lambda i, c=c: (0, c)),
            input_output_aliases=aliases,
            scratch_shapes=[pltpu.VMEM((chunk, width), F32)],
            name="output",
        compiler_params=vmem(20),
            cost_estimate=cost(2 * chunk * width * width, 0, 6_000_000),
        )(*operands)
    return out.T.reshape(1, suf, part)


def solution(mesh):
    in_specs = (
        P("req", None, None),
        P("req"),
        P("req"),
        P(),
        P("req", "tp", None),
        P(None, "tp"),
        P(None, "tp"),
        P(None, "tp"),
        P("tp", None),
        P("tp", None),
        P(),
    )
    out_specs = P("req", None, "tp")
    return jax.shard_map(local, mesh=mesh, in_specs=in_specs, out_specs=out_specs, check_vma=False)
```

```python
import math

import jax
import jax.numpy as jnp
import numpy as np
from jax import lax
from jax.experimental import pallas as pl
from jax.experimental.pallas import tpu as pltpu
from jax.sharding import PartitionSpec as P


F32 = jnp.float32
BF16 = jnp.bfloat16
LOG2E = math.log2(math.e)
EPS = 1e-06

NX, NZ, NY = 2, 8, 4


def add3(a, b):
    return ((a[0] + b[0]) % NX, (a[1] + b[1]) % NZ, (a[2] + b[2]) % NY)


def flat3(a):
    return a[0] * NZ * NY + a[1] * NY + a[2]


def unflat3(i):
    return (i // (NZ * NY), (i // NY) % NZ, i % NY)


def fetch(array, offset):
    pairs = [(flat3(add3(unflat3(i), offset)), i) for i in range(NX * NZ * NY)]
    return lax.ppermute(array, "req", pairs)


QUAD = ((0, 0, 0), (1, 0, 0), (0, 4, 0), (1, 4, 0))
HALVES = (
    dict(
        pool=((0, 0, 0), (0, 1, 0), (0, 7, 0), (0, 6, 0)),
        near=((0, 0, 1), (0, 0, 3), (0, 0, 2)),
        sends=((0, 0, 1), (0, 0, 3), (0, 0, 2)),
    ),
    dict(
        pool=((0, 0, 0), (0, 0, 1), (0, 0, 3), (0, 0, 2)),
        near=((0, 1, 0), (0, 7, 0), (0, 2, 0)),
        sends=((0, 1, 0), (0, 7, 0), (0, 2, 0), (0, 6, 0)),
    ),
)
CAP = 8
SMALL = 64
CHUNKS = 2


def minus3(a):
    return (-a[0] % NX, -a[1] % NZ, -a[2] % NY)


def place_table(half):
    pool = [add3(p, q) for p in half["pool"] for q in QUAD]
    order = [add3(n, m) for n in ((0, 0, 0),) + half["near"] for m in pool]
    assert sorted(flat3(m) for m in order) == list(range(64))
    table = np.zeros(64, np.int32)
    for place, m in enumerate(order):
        table[flat3(m)] = place
    return table


def member_spot(target):
    for n, half in enumerate(HALVES):
        for k, p in enumerate(half["pool"]):
            for b, q in enumerate(QUAD):
                if add3(p, q) == target:
                    return n, k, b
    raise ValueError(target)


def dot_t(a, b):
    return lax.dot_general(a, b, (((1,), (1,)), ((), ())), preferred_element_type=F32)


def pair_lanes(scale, fill):
    return jnp.concatenate([scale, jnp.full_like(scale, fill)], axis=1)


def lane_half(lanes):
    return lax.broadcasted_iota(jnp.int32, (1, lanes), 1) < lanes // 2


def prep_kernel(member_ref, block_ref, scale_ref, flag_ref, whole_ref):
    heads, rows, lanes = block_ref.shape
    size = lanes // 2
    first = lane_half(lanes)
    scale = scale_ref[...]
    bound = jnp.max(scale * scale) * (1.02 * LOG2E * math.sqrt(size))
    flag_ref[0] = (bound <= 60.0).astype(jnp.int32)
    for h in range(heads):
        wide = block_ref[h].astype(F32)
        mean = jnp.sum(jnp.where(first, wide * wide, 0.0), axis=-1, keepdims=True) * (1.0 / size)
        keys = wide * lax.rsqrt(mean + EPS) * pair_lanes(scale[h : h + 1], 1.0)
        whole_ref[h] = jnp.where(first, keys, wide).astype(BF16)
    whole_ref[heads] = jnp.full((rows, lanes), member_ref[0].astype(F32)).astype(BF16)


def qkv_kernel(
    hid_hbm, wq_hbm, wk_hbm, wv_hbm, scale_ref, q_ref, kv_ref, hid_ref, w_ref, sems, *, tile
):
    heads, suf, lanes = q_ref.shape
    size = lanes // 2
    first = lane_half(lanes)
    tiles = suf // tile
    copies = [
        pltpu.make_async_copy(
            hid_hbm.at[pl.ds(i * tile, tile)], hid_ref.at[pl.ds(i * tile, tile)], sems.at[i]
        )
        for i in range(tiles)
    ]
    for h in range(heads):
        for n, (hbm, row) in enumerate(((wq_hbm, 0), (wk_hbm, 2 * size), (wv_hbm, 3 * size))):
            copies.append(
                pltpu.make_async_copy(
                    hbm.at[pl.ds(h * size, size)],
                    w_ref.at[h, pl.ds(row, size)],
                    sems.at[tiles + 3 * h + n],
                )
            )
    for copy in copies:
        copy.start()
    for h in range(heads):
        w_ref[h, size : 2 * size] = jnp.zeros((size, w_ref.shape[2]), BF16)
    for h in range(heads):
        for copy in copies[tiles + 3 * h : tiles + 3 * h + 3]:
            copy.wait()
        scale = scale_ref[h : h + 1]
        q_scale = pair_lanes(scale * (LOG2E / math.sqrt(size)), 0.0)
        k_scale = pair_lanes(scale, 1.0)
        for i in range(tiles):
            if h == 0:
                copies[i].wait()
            rows = slice(i * tile, (i + 1) * tile)
            both = dot_t(hid_ref[rows], w_ref[h])
            q, kv = both[:, :lanes], both[:, lanes:]
            q_mean = jnp.sum(q * q, axis=-1, keepdims=True) * (1.0 / size)
            k_mean = jnp.sum(jnp.where(first, kv * kv, 0.0), axis=-1, keepdims=True) * (1.0 / size)
            q_ref[h, rows] = (q * lax.rsqrt(q_mean + EPS) * q_scale).astype(BF16)
            keys = kv * lax.rsqrt(k_mean + EPS) * k_scale
            kv_ref[h, rows] = jnp.where(first, keys, kv).astype(BF16)


def suffix_kernel(len_ref, flag_ref, q_ref, kv_ref, acc_ref, *, tile):
    heads, suf, lanes = q_ref.shape
    first = lane_half(lanes)
    length = len_ref[0]
    safe = flag_ref[0] == 1

    @pl.when(safe)
    def _():
        qpos = lax.broadcasted_iota(jnp.int32, (tile, tile), 0)
        kpos = lax.broadcasted_iota(jnp.int32, (tile, tile), 1)
        masks = []
        for j in range(suf // tile):
            inside = kpos + j * tile < length
            masks.append((inside & (kpos <= qpos), inside))
        for h in range(heads):
            for i in range(suf // tile):
                rows = slice(i * tile, (i + 1) * tile)
                total = None
                for j in range(i + 1):
                    keys = kv_ref[h, j * tile : (j + 1) * tile]
                    weights = jnp.exp2(dot_t(q_ref[h, rows], keys))
                    weights = jnp.where(masks[j][0 if i == j else 1], weights, 0.0).astype(BF16)
                    ones_values = jnp.where(first, jnp.ones_like(keys), keys)
                    part = jnp.dot(weights, ones_values, preferred_element_type=F32)
                    total = part if total is None else total + part
                acc_ref[h, rows] = total

    @pl.when(jnp.logical_not(safe))
    def _():
        lane = lax.broadcasted_iota(jnp.int32, (1, lanes), 1)
        pieces = suf // SMALL

        def piece(n, carry):
            h = n // pieces
            row = pl.multiple_of((n % pieces) * SMALL, SMALL)
            rows = pl.ds(row, SMALL)
            qpos = lax.broadcasted_iota(jnp.int32, (SMALL, suf), 0) + row
            kpos = lax.broadcasted_iota(jnp.int32, (SMALL, suf), 1)
            keys = kv_ref[h]
            scores = jnp.where((kpos <= qpos) & (kpos < length), dot_t(q_ref[h, rows], keys), -1e30)
            peak = jnp.max(scores, axis=-1, keepdims=True)
            weights = jnp.exp2(scores - peak).astype(BF16)
            ones_values = jnp.where(first, jnp.ones_like(keys), keys)
            total = jnp.dot(weights, ones_values, preferred_element_type=F32)
            acc_ref[h, rows] = jnp.where(lane == 0, peak, total)
            return carry

        lax.fori_loop(0, heads * pieces, piece, 0)


def split_kernel(a_ref, b_ref, c_ref, d_ref, one_ref, two_ref):
    rows = one_ref.shape[2]
    for n, ref in enumerate((a_ref, b_ref, c_ref, d_ref)):
        one_ref[n] = ref[:, :rows]
        two_ref[n] = ref[:, rows:]


def plan_kernel(member_ref, place_ref, owners_ref, table_ref, send_ref, recv_ref, over_ref, count_ref):
    group = member_ref[0]
    me = place_ref[0]
    groups, slots = owners_ref.shape

    def spots(owner):
        rel = (
            ((owner ^ me) & 32)
            + ((((owner >> 2) - (me >> 2)) & 7) << 2)
            + ((owner - me) & 3)
        )
        return table_ref[rel], table_ref[64 + rel]

    def by_group(g, most):
        for n in range(8):
            count_ref[n] = 0

        def by_slot(j, carry):
            most, held = carry
            owner = owners_ref[g, j]
            after = []
            for half, (spot, color) in enumerate(zip(spots(owner), (owner & 3, (owner >> 2) & 3))):
                send_ref[half * 64 + g * slots + held[half]] = spot
                after.append(held[half] + (spot < 16).astype(jnp.int32))
                seen = count_ref[half * 4 + color] + 1
                count_ref[half * 4 + color] = seen
                most = jnp.maximum(most, seen)
            return most, tuple(after)

        return lax.fori_loop(0, slots, by_slot, (most, (jnp.int32(0), jnp.int32(0))))[0]

    most = lax.fori_loop(0, groups, by_group, jnp.int32(0))
    over_ref[0] = (most > CAP).astype(jnp.int32)
    for n in range(8):
        count_ref[n] = 0

    def by_own(j, carry):
        for half, spot in enumerate(spots(owners_ref[group, j])):
            source = spot >> 4
            rank = count_ref[half * 4 + source]
            count_ref[half * 4 + source] = rank + 1
            recv_ref[half * slots + j] = source * 16 + rank
        return carry

    lax.fori_loop(0, slots, by_own, 0)


def pack_kernel(member_ref, send_ref, *rest, start):
    quads, outs, pool_ref = (rest[:4], rest[4:8]), rest[8:-1], rest[-1]
    heads = pool_ref.shape[2]
    for half in range(2):
        for n in range(4):
            pool_ref[half, 4 * n : 4 * n + 4] = quads[half][n][:, :heads]

    def wanted(target):
        n, k, b = member_spot(target)
        value = quads[n][k][b, heads].astype(F32)
        return jnp.max(value).astype(jnp.int32)

    jobs = []
    place = 0
    for n, half in enumerate(HALVES):
        if start == 0:
            jobs.append((outs[place], n, member_ref[0], 0))
            place += 1
        for k, offset in enumerate(half["sends"]):
            out = outs[place]
            place += 1
            jobs.append((out, n, wanted(minus3(offset)), start + (out.shape[0] if k == 3 else 0)))
    for out, half, group, first in jobs:

        def copy(i, carry, out=out, half=half, group=group, first=first):
            spot = send_ref[half * 64 + group * 16 + first + i] & 15
            out[i] = pool_ref[half, spot]
            return carry

        lax.fori_loop(0, out.shape[0], copy, 0)


def select_kernel(recv_ref, *rest):
    kv_ref, sems = rest[-2:]
    blocks = rest[:-2]
    slots = recv_ref.shape[0] // 2
    part = kv_ref.shape[1] // (2 * slots)
    spots = []
    for start in range(0, CAP * (2 if len(blocks) > 9 else 1), CAP):
        for n, half in enumerate(HALVES):
            if start == 0:
                spots.append((n, 0, 0))
            for k in range(len(half["sends"])):
                spots.append((n, min(k, 2) + 1, start + (CAP // 2 if k == 3 else 0)))
    assert len(spots) == len(blocks)

    def begin(j, carry):
        for half in range(2):
            code = recv_ref[half * slots + j]
            row = pl.multiple_of((2 * j + half) * part, part)
            goal = kv_ref.at[:, pl.ds(row, part), :]
            for ref, (n, source, low) in zip(blocks, spots):
                if n != half:
                    continue
                least = source * 16 + low

                @pl.when((code >= least) & (code < least + ref.shape[0]))
                def _(ref=ref, least=least):
                    pltpu.make_async_copy(ref.at[code - least], goal, sems.at[2 * j + half]).start()

        return carry

    lax.fori_loop(0, slots, begin, 0)

    def finish(j, carry):
        row = pl.multiple_of(j * part, part)
        goal = kv_ref.at[:, pl.ds(row, part), :]
        pltpu.make_async_copy(blocks[0].at[0], goal, sems.at[j]).wait()
        return carry

    lax.fori_loop(0, 2 * slots, finish, 0)


def attend_kernel(
    flag_ref, q_hbm, acc_hbm, kv_hbm, out_ref, q_ref, acc_ref, kv_ref, total_ref, sems, *, tile, start
):
    heads, rows, lanes = q_ref.shape
    size = lanes // 2
    count = kv_ref.shape[1]
    first = lane_half(lanes)
    safe = flag_ref[0] == 1
    own = pl.ds(start, rows)
    copies = [
        (
            pltpu.make_async_copy(q_hbm.at[h, own], q_ref.at[h], sems.at[3 * h]),
            pltpu.make_async_copy(kv_hbm.at[h], kv_ref.at[h], sems.at[3 * h + 1]),
            pltpu.make_async_copy(acc_hbm.at[h, own], acc_ref.at[h], sems.at[3 * h + 2]),
        )
        for h in range(heads)
    ]
    for copy in copies:
        for one in copy:
            one.start()

    @pl.when(safe)
    def _():
        for h in range(heads):
            for one in copies[h]:
                one.wait()
            total = acc_ref[h]
            for j in range(count // tile):
                keys = kv_ref[h, j * tile : (j + 1) * tile]
                weights = jnp.exp2(dot_t(q_ref[h], keys)).astype(BF16)
                ones_values = jnp.where(first, jnp.ones_like(keys), keys)
                total = total + jnp.dot(weights, ones_values, preferred_element_type=F32)
            value = total / pltpu.roll(total, size, 1)
            out_ref[:, h * size : (h + 1) * size] = value[:, size:].astype(BF16)

    @pl.when(jnp.logical_not(safe))
    def _():
        for copy in copies:
            for one in copy:
                one.wait()

        pieces = rows // SMALL

        def piece(n, carry):
            h = n // pieces
            part = pl.ds(pl.multiple_of((n % pieces) * SMALL, SMALL), SMALL)
            keys = kv_ref[h]
            held = acc_ref[h, part]
            near = held[:, :1]
            held = jnp.where(first, held[:, 1:2], held)
            scores = dot_t(q_ref[h, part], keys)
            peak = jnp.maximum(jnp.max(scores, axis=-1, keepdims=True), near)
            weights = jnp.exp2(scores - peak).astype(BF16)
            ones_values = jnp.where(first, jnp.ones_like(keys), keys)
            total = jnp.dot(weights, ones_values, preferred_element_type=F32)
            total_ref[h, part] = total + held * jnp.exp2(near - peak)
            return carry

        lax.fori_loop(0, heads * pieces, piece, 0)
        for h in range(heads):
            total = total_ref[h]
            value = total / pltpu.roll(total, size, 1)
            out_ref[:, h * size : (h + 1) * size] = value[:, size:].astype(BF16)


def output_kernel(
    len_ref, rank_ref, a0, a1, a2, a3, w0, w1, w2, w3, hid_ref, rate_ref, *rest, tile, start
):
    out_ref, moved_ref, w_ref, sems = rest[-4:]
    count, width = hid_ref.shape
    part = out_ref.shape[0]
    length = len_ref[0]
    rank = rank_ref[0]
    cols = [slice(n * tile, (n + 1) * tile) for n in range(width // tile)]
    copies = [
        [
            pltpu.make_async_copy(w.at[:, pl.ds(n * tile, tile)], w_ref.at[k, n], sems.at[4 * n + k])
            for k, w in enumerate((w0, w1, w2, w3))
        ]
        for n in range(len(cols))
    ]
    for group in copies:
        for copy in group:
            copy.start()
    square = None
    for n, col in enumerate(cols):
        for copy in copies[n]:
            copy.wait()
        branch = jnp.dot(a0[...], w_ref[0, n], preferred_element_type=F32)
        for k, a in ((1, a1), (2, a2), (3, a3)):
            branch += jnp.dot(a[...], w_ref[k, n], preferred_element_type=F32)
        moved_ref[:, col] = branch
        part_square = jnp.sum(branch * branch, axis=-1, keepdims=True)
        square = part_square if square is None else square + part_square
    gain = lax.rsqrt(square * (1.0 / width) + EPS)
    square = None
    for col in cols:
        state = hid_ref[:, col].astype(F32)
        moved = state + rate_ref[:, col] * (moved_ref[:, col] * gain - state)
        moved_ref[:, col] = moved
        part_square = jnp.sum(moved * moved, axis=-1, keepdims=True)
        square = part_square if square is None else square + part_square
    norm = lax.rsqrt(square * (1.0 / width) + EPS)
    pos = lax.broadcasted_iota(jnp.int32, (count, 1), 0) + start
    for t in range(width // part):

        @pl.when(rank == t)
        def _(t=t):
            mine = moved_ref[:, t * part : (t + 1) * part]
            out_ref[...] = jnp.where(pos < length, mine * norm, 0.0).T.astype(BF16)


VMEM = pl.BlockSpec(memory_space=pltpu.VMEM)
SMEM = pl.BlockSpec(memory_space=pltpu.SMEM)
ANY = pl.BlockSpec(memory_space=pl.ANY)
HBM = pl.BlockSpec(memory_space=pltpu.HBM)


def across(array, bit):
    return lax.ppermute(array, "tp", [(i, i ^ bit) for i in range(4)])


def shaped(shape, dtype):
    return jax.ShapeDtypeStruct(shape, dtype)


def vmem(mebibytes):
    return pltpu.CompilerParams(vmem_limit_bytes=mebibytes << 20)


def cost(flops, exps, moved):
    return pl.CostEstimate(flops=flops, transcendentals=exps, bytes_accessed=moved)


def gather_prefix(whole, membership, owners):
    planes, rows, lanes = whole.shape
    heads, part, slots = planes - 1, rows // 2, owners.shape[1]
    place = lax.axis_index("req").astype(jnp.int32).reshape(1)
    table = jnp.asarray(np.concatenate([place_table(half) for half in HALVES]))
    send, recv, over = pl.pallas_call(
        plan_kernel,
        out_shape=(shaped((128,), jnp.int32), shaped((2 * slots,), jnp.int32), shaped((1,), jnp.int32)),
        in_specs=[SMEM] * 4,
        out_specs=(SMEM,) * 3,
        scratch_shapes=[pltpu.SMEM((8,), jnp.int32)],
        name="plan",
        compiler_params=vmem(1),
        cost_estimate=cost(0, 0, 1_000_000),
    )(membership, place, owners, table)
    quads = pl.pallas_call(
        split_kernel,
        out_shape=(shaped((4, planes, part, lanes), BF16),) * 2,
        in_specs=[VMEM] * 4,
        out_specs=(VMEM, VMEM),
        name="split",
        compiler_params=vmem(2),
        cost_estimate=cost(0, 0, 600_000),
    )(whole, *[fetch(whole, offset) for offset in QUAD[1:]])
    held = []
    for quad, half in zip(quads, HALVES):
        held += [quad] + [fetch(quad, offset) for offset in half["pool"][1:]]

    def one_round(start):
        shapes, offsets = [], []
        for half in HALVES:
            if start == 0:
                shapes.append(16)
                offsets.append(None)
            for offset in half["sends"]:
                shapes.append(CAP // 2 if len(half["sends"]) == 4 and offset[1] in (2, 6) else CAP)
                offsets.append(offset)
        packed = pl.pallas_call(
            lambda *refs: pack_kernel(*refs, start=start),
            out_shape=tuple(shaped((n, heads, part, lanes), BF16) for n in shapes),
            in_specs=[SMEM] * 2 + [VMEM] * 8,
            out_specs=(VMEM,) * len(shapes),
            scratch_shapes=[pltpu.VMEM((2, 16, heads, part, lanes), BF16)],
            name="pack",
            compiler_params=vmem(8),
            cost_estimate=cost(0, 0, 4_000_000),
        )(membership, send, *held)
        return [a if o is None else fetch(a, o) for a, o in zip(packed, offsets)]

    def select(arrays):
        return pl.pallas_call(
            select_kernel,
            out_shape=shaped((heads, slots * rows, lanes), BF16),
            in_specs=[SMEM] + [ANY] * len(arrays),
            out_specs=VMEM,
            scratch_shapes=[pltpu.SemaphoreType.DMA((2 * slots,))],
            name="select",
            compiler_params=vmem(4),
            cost_estimate=cost(0, 0, 3_000_000),
        )(recv, *arrays)

    arrays = one_round(0)
    prefix = lax.cond(
        over[0] > 0,
        lambda: select(arrays + one_round(CAP)),
        lambda: select(arrays),
    )
    return prefix


def local(
    hidden,
    membership,
    lengths,
    owners,
    prefix_cache,
    w_query,
    w_key,
    w_value,
    key_scale,
    w_out,
    step_rates,
):
    _, suf, width = hidden.shape
    heads, size = key_scale.shape
    lanes = 2 * size
    slot_rows = prefix_cache.shape[0]
    rows = hidden.reshape(suf, width)
    flag, whole = pl.pallas_call(
        prep_kernel,
        out_shape=(shaped((1,), jnp.int32), shaped((heads + 1, slot_rows, lanes), BF16)),
        in_specs=[SMEM, VMEM, VMEM],
        out_specs=(SMEM, VMEM),
        name="prep",
        compiler_params=vmem(2),
        cost_estimate=cost(0, 0, 300_000),
    )(membership, jnp.transpose(prefix_cache, (1, 0, 2)), key_scale)
    prefix = gather_prefix(whole, membership, owners)
    w_far = across(w_out, 2)
    q, kv = pl.pallas_call(
        lambda *refs: qkv_kernel(*refs, tile=256),
        out_shape=(shaped((heads, suf, lanes), BF16),) * 2,
        in_specs=[HBM] * 4 + [VMEM],
        out_specs=(VMEM, VMEM),
        scratch_shapes=[
            pltpu.VMEM((suf, width), BF16),
            pltpu.VMEM((heads, 2 * lanes, width), BF16),
            pltpu.SemaphoreType.DMA((2 + 3 * heads,)),
        ],
        name="qkv",
        compiler_params=vmem(14),
        cost_estimate=cost(2 * suf * width * 3 * heads * size, 0, 10_000_000),
    )(rows, w_query.T, w_key.T, w_value.T, key_scale)
    acc = pl.pallas_call(
        lambda *refs: suffix_kernel(*refs, tile=256),
        out_shape=shaped((heads, suf, lanes), F32),
        in_specs=[SMEM, SMEM, VMEM, VMEM],
        out_specs=VMEM,
        name="suffix",
        compiler_params=vmem(10),
        cost_estimate=cost(4 * suf * suf * heads * lanes, suf * suf * heads, 10_000_000),
    )(lengths, flag, q, kv)
    w_core = across(w_out, 1)
    w_both = across(w_far, 1)
    prefix_rows = prefix.shape[1]
    part = width // 4
    rank = lax.axis_index("tp").astype(jnp.int32).reshape(1)
    chunk = suf // CHUNKS
    attended = []
    for c in range(CHUNKS):
        attended.append(
            pl.pallas_call(
                lambda *refs, c=c: attend_kernel(*refs, tile=256, start=c * chunk),
                out_shape=shaped((chunk, heads * size), BF16),
                in_specs=[SMEM, ANY, ANY, ANY],
                out_specs=VMEM,
                scratch_shapes=[
                    pltpu.VMEM((heads, chunk, lanes), BF16),
                    pltpu.VMEM((heads, chunk, lanes), F32),
                    pltpu.VMEM((heads, prefix_rows, lanes), BF16),
                    pltpu.VMEM((heads, chunk, lanes), F32),
                    pltpu.SemaphoreType.DMA((3 * heads,)),
                ],
                name="attend",
                compiler_params=vmem(10),
                cost_estimate=cost(4 * chunk * prefix_rows * heads * lanes, chunk * prefix_rows * heads, 8_000_000),
            )(flag, q, acc, prefix)
        )
    out = None
    for c in range(CHUNKS):
        far = across(attended[c], 2)
        core = across(attended[c], 1)
        both = across(attended[c], 3)
        operands = [lengths, rank, attended[c], core, far, both, w_out, w_core, w_far, w_both, rows, step_rates.reshape(1, width)]
        specs = [SMEM] * 2 + [VMEM] * 4 + [HBM] * 4 + [pl.BlockSpec((chunk, width), lambda i, c=c: (c, 0)), VMEM]
        aliases = {}
        if out is not None:
            aliases = {len(operands): 0}
            operands.append(out)
            specs.append(ANY)
        out = pl.pallas_call(
            lambda *refs, c=c: output_kernel(*refs, tile=256, start=c * chunk),
            grid=(1,),
            out_shape=shaped((part, suf), BF16),
            in_specs=specs,
            out_specs=pl.BlockSpec((part, chunk), lambda i, c=c: (0, c)),
            input_output_aliases=aliases,
            scratch_shapes=[
                pltpu.VMEM((chunk, width), F32),
                pltpu.VMEM((4, width // 256, heads * size, 256), BF16),
                pltpu.SemaphoreType.DMA((4 * (width // 256),)),
            ],
            name="output",
        compiler_params=vmem(20),
            cost_estimate=cost(2 * chunk * width * width, 0, 6_000_000),
        )(*operands)
    return out.T.reshape(1, suf, part)


def solution(mesh):
    in_specs = (
        P("req", None, None),
        P("req"),
        P("req"),
        P(),
        P("req", "tp", None),
        P(None, "tp"),
        P(None, "tp"),
        P(None, "tp"),
        P("tp", None),
        P("tp", None),
        P(),
    )
    out_specs = P("req", None, "tp")
    return jax.shard_map(local, mesh=mesh, in_specs=in_specs, out_specs=out_specs, check_vma=False)
```

```python
import math

import jax
import jax.numpy as jnp
import numpy as np
from jax import lax
from jax.experimental import pallas as pl
from jax.experimental.pallas import tpu as pltpu
from jax.sharding import PartitionSpec as P


F32 = jnp.float32
BF16 = jnp.bfloat16
LOG2E = math.log2(math.e)
EPS = 1e-06

NX, NZ, NY = 2, 8, 4


def add3(a, b):
    return ((a[0] + b[0]) % NX, (a[1] + b[1]) % NZ, (a[2] + b[2]) % NY)


def flat3(a):
    return a[0] * NZ * NY + a[1] * NY + a[2]


def unflat3(i):
    return (i // (NZ * NY), (i // NY) % NZ, i % NY)


def fetch(array, offset):
    pairs = [(flat3(add3(unflat3(i), offset)), i) for i in range(NX * NZ * NY)]
    return lax.ppermute(array, "req", pairs)


QUAD = ((0, 0, 0), (1, 0, 0), (0, 4, 0), (1, 4, 0))
HALVES = (
    dict(
        pool=((0, 0, 0), (0, 1, 0), (0, 7, 0), (0, 6, 0)),
        near=((0, 0, 1), (0, 0, 3), (0, 0, 2)),
        sends=((0, 0, 1), (0, 0, 3), (0, 0, 2)),
    ),
    dict(
        pool=((0, 0, 0), (0, 0, 1), (0, 0, 3), (0, 0, 2)),
        near=((0, 1, 0), (0, 7, 0), (0, 2, 0)),
        sends=((0, 1, 0), (0, 7, 0), (0, 2, 0), (0, 6, 0)),
    ),
)
CAP = 8
SMALL = 64
CHUNKS = 2


def minus3(a):
    return (-a[0] % NX, -a[1] % NZ, -a[2] % NY)


def place_table(half):
    pool = [add3(p, q) for p in half["pool"] for q in QUAD]
    order = [add3(n, m) for n in ((0, 0, 0),) + half["near"] for m in pool]
    assert sorted(flat3(m) for m in order) == list(range(64))
    table = np.zeros(64, np.int32)
    for place, m in enumerate(order):
        table[flat3(m)] = place
    return table


def member_spot(target):
    for n, half in enumerate(HALVES):
        for k, p in enumerate(half["pool"]):
            for b, q in enumerate(QUAD):
                if add3(p, q) == target:
                    return n, k, b
    raise ValueError(target)


def dot_t(a, b):
    return lax.dot_general(a, b, (((1,), (1,)), ((), ())), preferred_element_type=F32)


def pair_lanes(scale, fill):
    return jnp.concatenate([scale, jnp.full_like(scale, fill)], axis=1)


def lane_half(lanes):
    return lax.broadcasted_iota(jnp.int32, (1, lanes), 1) < lanes // 2


def prep_kernel(member_ref, block_ref, scale_ref, flag_ref, whole_ref):
    heads, rows, lanes = block_ref.shape
    size = lanes // 2
    first = lane_half(lanes)
    scale = scale_ref[...]
    bound = jnp.max(scale * scale) * (1.02 * LOG2E * math.sqrt(size))
    flag_ref[0] = (bound <= 60.0).astype(jnp.int32)
    for h in range(heads):
        wide = block_ref[h].astype(F32)
        mean = jnp.sum(jnp.where(first, wide * wide, 0.0), axis=-1, keepdims=True) * (1.0 / size)
        keys = wide * lax.rsqrt(mean + EPS) * pair_lanes(scale[h : h + 1], 1.0)
        whole_ref[h] = jnp.where(first, keys, wide).astype(BF16)
    whole_ref[heads] = jnp.full((rows, lanes), member_ref[0].astype(F32)).astype(BF16)


def qkv_kernel(hid_ref, wq_ref, wk_ref, wv_ref, scale_ref, q_ref, kv_ref, w_ref, *, tile):
    heads, suf, lanes = q_ref.shape
    size = lanes // 2
    first = lane_half(lanes)
    for h in range(heads):
        own = slice(h * size, (h + 1) * size)
        w_ref[h, :size] = wq_ref[own]
        w_ref[h, size : 2 * size] = jnp.zeros_like(wq_ref[own])
        w_ref[h, 2 * size : 3 * size] = wk_ref[own]
        w_ref[h, 3 * size :] = wv_ref[own]
    for h in range(heads):
        scale = scale_ref[h : h + 1]
        q_scale = pair_lanes(scale * (LOG2E / math.sqrt(size)), 0.0)
        k_scale = pair_lanes(scale, 1.0)
        for i in range(suf // tile):
            rows = slice(i * tile, (i + 1) * tile)
            both = dot_t(hid_ref[rows], w_ref[h])
            q, kv = both[:, :lanes], both[:, lanes:]
            q_mean = jnp.sum(q * q, axis=-1, keepdims=True) * (1.0 / size)
            k_mean = jnp.sum(jnp.where(first, kv * kv, 0.0), axis=-1, keepdims=True) * (1.0 / size)
            q_ref[h, rows] = (q * lax.rsqrt(q_mean + EPS) * q_scale).astype(BF16)
            keys = kv * lax.rsqrt(k_mean + EPS) * k_scale
            kv_ref[h, rows] = jnp.where(first, keys, kv).astype(BF16)


def suffix_kernel(len_ref, flag_ref, q_ref, kv_ref, acc_ref, *, tile):
    heads, suf, lanes = q_ref.shape
    first = lane_half(lanes)
    length = len_ref[0]
    safe = flag_ref[0] == 1

    @pl.when(safe)
    def _():
        qpos = lax.broadcasted_iota(jnp.int32, (tile, tile), 0)
        kpos = lax.broadcasted_iota(jnp.int32, (tile, tile), 1)
        masks = []
        for j in range(suf // tile):
            inside = kpos + j * tile < length
            masks.append((inside & (kpos <= qpos), inside))
        for h in range(heads):
            for i in range(suf // tile):
                rows = slice(i * tile, (i + 1) * tile)
                total = None
                for j in range(i + 1):
                    keys = kv_ref[h, j * tile : (j + 1) * tile]
                    weights = jnp.exp2(dot_t(q_ref[h, rows], keys))
                    weights = jnp.where(masks[j][0 if i == j else 1], weights, 0.0).astype(BF16)
                    ones_values = jnp.where(first, jnp.ones_like(keys), keys)
                    part = jnp.dot(weights, ones_values, preferred_element_type=F32)
                    total = part if total is None else total + part
                acc_ref[h, rows] = total

    @pl.when(jnp.logical_not(safe))
    def _():
        lane = lax.broadcasted_iota(jnp.int32, (1, lanes), 1)
        pieces = suf // SMALL

        def piece(n, carry):
            h = n // pieces
            row = pl.multiple_of((n % pieces) * SMALL, SMALL)
            rows = pl.ds(row, SMALL)
            qpos = lax.broadcasted_iota(jnp.int32, (SMALL, suf), 0) + row
            kpos = lax.broadcasted_iota(jnp.int32, (SMALL, suf), 1)
            keys = kv_ref[h]
            scores = jnp.where((kpos <= qpos) & (kpos < length), dot_t(q_ref[h, rows], keys), -1e30)
            peak = jnp.max(scores, axis=-1, keepdims=True)
            weights = jnp.exp2(scores - peak).astype(BF16)
            ones_values = jnp.where(first, jnp.ones_like(keys), keys)
            total = jnp.dot(weights, ones_values, preferred_element_type=F32)
            acc_ref[h, rows] = jnp.where(lane == 0, peak, total)
            return carry

        lax.fori_loop(0, heads * pieces, piece, 0)


def split_kernel(a_ref, b_ref, c_ref, d_ref, one_ref, two_ref):
    rows = one_ref.shape[2]
    for n, ref in enumerate((a_ref, b_ref, c_ref, d_ref)):
        one_ref[n] = ref[:, :rows]
        two_ref[n] = ref[:, rows:]


def plan_kernel(member_ref, place_ref, owners_ref, table_ref, send_ref, recv_ref, over_ref, count_ref):
    group = member_ref[0]
    me = place_ref[0]
    groups, slots = owners_ref.shape

    def spots(owner):
        rel = (
            ((owner ^ me) & 32)
            + ((((owner >> 2) - (me >> 2)) & 7) << 2)
            + ((owner - me) & 3)
        )
        return table_ref[rel], table_ref[64 + rel]

    def by_group(g, most):
        for n in range(8):
            count_ref[n] = 0

        def by_slot(j, carry):
            most, held = carry
            owner = owners_ref[g, j]
            after = []
            for half, (spot, color) in enumerate(zip(spots(owner), (owner & 3, (owner >> 2) & 3))):
                send_ref[half * 64 + g * slots + held[half]] = spot
                after.append(held[half] + (spot < 16).astype(jnp.int32))
                seen = count_ref[half * 4 + color] + 1
                count_ref[half * 4 + color] = seen
                most = jnp.maximum(most, seen)
            return most, tuple(after)

        return lax.fori_loop(0, slots, by_slot, (most, (jnp.int32(0), jnp.int32(0))))[0]

    most = lax.fori_loop(0, groups, by_group, jnp.int32(0))
    over_ref[0] = (most > CAP).astype(jnp.int32)
    for n in range(8):
        count_ref[n] = 0

    def by_own(j, carry):
        for half, spot in enumerate(spots(owners_ref[group, j])):
            source = spot >> 4
            rank = count_ref[half * 4 + source]
            count_ref[half * 4 + source] = rank + 1
            recv_ref[half * slots + j] = source * 16 + rank
        return carry

    lax.fori_loop(0, slots, by_own, 0)


def pack_kernel(member_ref, send_ref, *rest, start):
    quads, outs, pool_ref = (rest[:4], rest[4:8]), rest[8:-1], rest[-1]
    heads = pool_ref.shape[2]
    for half in range(2):
        for n in range(4):
            pool_ref[half, 4 * n : 4 * n + 4] = quads[half][n][:, :heads]

    def wanted(target):
        n, k, b = member_spot(target)
        value = quads[n][k][b, heads].astype(F32)
        return jnp.max(value).astype(jnp.int32)

    jobs = []
    place = 0
    for n, half in enumerate(HALVES):
        if start == 0:
            jobs.append((outs[place], n, member_ref[0], 0))
            place += 1
        for k, offset in enumerate(half["sends"]):
            out = outs[place]
            place += 1
            jobs.append((out, n, wanted(minus3(offset)), start + (out.shape[0] if k == 3 else 0)))
    for out, half, group, first in jobs:

        def copy(i, carry, out=out, half=half, group=group, first=first):
            spot = send_ref[half * 64 + group * 16 + first + i] & 15
            out[i] = pool_ref[half, spot]
            return carry

        lax.fori_loop(0, out.shape[0], copy, 0)


def select_kernel(recv_ref, *rest):
    kv_ref, sems = rest[-2:]
    blocks = rest[:-2]
    slots = recv_ref.shape[0] // 2
    part = kv_ref.shape[1] // (2 * slots)
    spots = []
    for start in range(0, CAP * (2 if len(blocks) > 9 else 1), CAP):
        for n, half in enumerate(HALVES):
            if start == 0:
                spots.append((n, 0, 0))
            for k in range(len(half["sends"])):
                spots.append((n, min(k, 2) + 1, start + (CAP // 2 if k == 3 else 0)))
    assert len(spots) == len(blocks)

    def begin(j, carry):
        for half in range(2):
            code = recv_ref[half * slots + j]
            row = pl.multiple_of((2 * j + half) * part, part)
            goal = kv_ref.at[:, pl.ds(row, part), :]
            for ref, (n, source, low) in zip(blocks, spots):
                if n != half:
                    continue
                least = source * 16 + low

                @pl.when((code >= least) & (code < least + ref.shape[0]))
                def _(ref=ref, least=least):
                    pltpu.make_async_copy(ref.at[code - least], goal, sems.at[2 * j + half]).start()

        return carry

    lax.fori_loop(0, slots, begin, 0)

    def finish(j, carry):
        row = pl.multiple_of(j * part, part)
        goal = kv_ref.at[:, pl.ds(row, part), :]
        pltpu.make_async_copy(blocks[0].at[0], goal, sems.at[j]).wait()
        return carry

    lax.fori_loop(0, 2 * slots, finish, 0)


def attend_kernel(flag_ref, q_ref, acc_ref, kv_ref, out_ref, total_ref, *, tile):
    heads, rows, lanes = q_ref.shape
    size = lanes // 2
    count = kv_ref.shape[1]
    first = lane_half(lanes)
    safe = flag_ref[0] == 1

    @pl.when(safe)
    def _():
        for h in range(heads):
            total = acc_ref[h]
            for j in range(count // tile):
                keys = kv_ref[h, j * tile : (j + 1) * tile]
                weights = jnp.exp2(dot_t(q_ref[h], keys)).astype(BF16)
                ones_values = jnp.where(first, jnp.ones_like(keys), keys)
                total = total + jnp.dot(weights, ones_values, preferred_element_type=F32)
            total_ref[h] = total

    @pl.when(jnp.logical_not(safe))
    def _():
        pieces = rows // SMALL

        def piece(n, carry):
            h = n // pieces
            part = pl.ds(pl.multiple_of((n % pieces) * SMALL, SMALL), SMALL)
            keys = kv_ref[h]
            held = acc_ref[h, part]
            near = held[:, :1]
            held = jnp.where(first, held[:, 1:2], held)
            scores = dot_t(q_ref[h, part], keys)
            peak = jnp.maximum(jnp.max(scores, axis=-1, keepdims=True), near)
            weights = jnp.exp2(scores - peak).astype(BF16)
            ones_values = jnp.where(first, jnp.ones_like(keys), keys)
            total = jnp.dot(weights, ones_values, preferred_element_type=F32)
            total_ref[h, part] = total + held * jnp.exp2(near - peak)
            return carry

        lax.fori_loop(0, heads * pieces, piece, 0)

    for h in range(heads):
        total = total_ref[h]
        value = total / pltpu.roll(total, size, 1)
        out_ref[:, h * size : (h + 1) * size] = value[:, size:].astype(BF16)


def output_kernel(
    len_ref, rank_ref, a0, a1, a2, a3, w0, w1, w2, w3, hid_ref, rate_ref, *rest, tile, start
):
    out_ref, moved_ref = rest[-2:]
    count, width = hid_ref.shape
    part = out_ref.shape[0]
    length = len_ref[0]
    rank = rank_ref[0]
    cols = [slice(n * tile, (n + 1) * tile) for n in range(width // tile)]
    square = None
    for col in cols:
        branch = jnp.dot(a0[...], w0[:, col], preferred_element_type=F32)
        for a, w in ((a1, w1), (a2, w2), (a3, w3)):
            branch += jnp.dot(a[...], w[:, col], preferred_element_type=F32)
        moved_ref[:, col] = branch
        part_square = jnp.sum(branch * branch, axis=-1, keepdims=True)
        square = part_square if square is None else square + part_square
    gain = lax.rsqrt(square * (1.0 / width) + EPS)
    square = None
    for col in cols:
        state = hid_ref[:, col].astype(F32)
        moved = state + rate_ref[:, col] * (moved_ref[:, col] * gain - state)
        moved_ref[:, col] = moved
        part_square = jnp.sum(moved * moved, axis=-1, keepdims=True)
        square = part_square if square is None else square + part_square
    norm = lax.rsqrt(square * (1.0 / width) + EPS)
    pos = lax.broadcasted_iota(jnp.int32, (count, 1), 0) + start
    for t in range(width // part):

        @pl.when(rank == t)
        def _(t=t):
            mine = moved_ref[:, t * part : (t + 1) * part]
            out_ref[...] = jnp.where(pos < length, mine * norm, 0.0).T.astype(BF16)


VMEM = pl.BlockSpec(memory_space=pltpu.VMEM)
SMEM = pl.BlockSpec(memory_space=pltpu.SMEM)
ANY = pl.BlockSpec(memory_space=pl.ANY)


def across(array, bit):
    return lax.ppermute(array, "tp", [(i, i ^ bit) for i in range(4)])


def shaped(shape, dtype):
    return jax.ShapeDtypeStruct(shape, dtype)


def vmem(mebibytes):
    return pltpu.CompilerParams(vmem_limit_bytes=mebibytes << 20)


def cost(flops, exps, moved):
    return pl.CostEstimate(flops=flops, transcendentals=exps, bytes_accessed=moved)


def gather_prefix(whole, membership, owners):
    planes, rows, lanes = whole.shape
    heads, part, slots = planes - 1, rows // 2, owners.shape[1]
    place = lax.axis_index("req").astype(jnp.int32).reshape(1)
    table = jnp.asarray(np.concatenate([place_table(half) for half in HALVES]))
    send, recv, over = pl.pallas_call(
        plan_kernel,
        out_shape=(shaped((128,), jnp.int32), shaped((2 * slots,), jnp.int32), shaped((1,), jnp.int32)),
        in_specs=[SMEM] * 4,
        out_specs=(SMEM,) * 3,
        scratch_shapes=[pltpu.SMEM((8,), jnp.int32)],
        name="plan",
        compiler_params=vmem(1),
        cost_estimate=cost(0, 0, 1_000_000),
    )(membership, place, owners, table)
    quads = pl.pallas_call(
        split_kernel,
        out_shape=(shaped((4, planes, part, lanes), BF16),) * 2,
        in_specs=[VMEM] * 4,
        out_specs=(VMEM, VMEM),
        name="split",
        compiler_params=vmem(2),
        cost_estimate=cost(0, 0, 600_000),
    )(whole, *[fetch(whole, offset) for offset in QUAD[1:]])
    held = []
    for quad, half in zip(quads, HALVES):
        held += [quad] + [fetch(quad, offset) for offset in half["pool"][1:]]

    def one_round(start):
        shapes, offsets = [], []
        for half in HALVES:
            if start == 0:
                shapes.append(16)
                offsets.append(None)
            for offset in half["sends"]:
                shapes.append(CAP // 2 if len(half["sends"]) == 4 and offset[1] in (2, 6) else CAP)
                offsets.append(offset)
        packed = pl.pallas_call(
            lambda *refs: pack_kernel(*refs, start=start),
            out_shape=tuple(shaped((n, heads, part, lanes), BF16) for n in shapes),
            in_specs=[SMEM] * 2 + [VMEM] * 8,
            out_specs=(VMEM,) * len(shapes),
            scratch_shapes=[pltpu.VMEM((2, 16, heads, part, lanes), BF16)],
            name="pack",
            compiler_params=vmem(8),
            cost_estimate=cost(0, 0, 4_000_000),
        )(membership, send, *held)
        return [a if o is None else fetch(a, o) for a, o in zip(packed, offsets)]

    def select(arrays):
        return pl.pallas_call(
            select_kernel,
            out_shape=shaped((heads, slots * rows, lanes), BF16),
            in_specs=[SMEM] + [ANY] * len(arrays),
            out_specs=VMEM,
            scratch_shapes=[pltpu.SemaphoreType.DMA((2 * slots,))],
            name="select",
            compiler_params=vmem(4),
            cost_estimate=cost(0, 0, 3_000_000),
        )(recv, *arrays)

    arrays = one_round(0)
    prefix = lax.cond(
        over[0] > 0,
        lambda: select(arrays + one_round(CAP)),
        lambda: select(arrays),
    )
    return prefix


def local(
    hidden,
    membership,
    lengths,
    owners,
    prefix_cache,
    w_query,
    w_key,
    w_value,
    key_scale,
    w_out,
    step_rates,
):
    _, suf, width = hidden.shape
    heads, size = key_scale.shape
    lanes = 2 * size
    slot_rows = prefix_cache.shape[0]
    rows = hidden.reshape(suf, width)
    flag, whole = pl.pallas_call(
        prep_kernel,
        out_shape=(shaped((1,), jnp.int32), shaped((heads + 1, slot_rows, lanes), BF16)),
        in_specs=[SMEM, VMEM, VMEM],
        out_specs=(SMEM, VMEM),
        name="prep",
        compiler_params=vmem(2),
        cost_estimate=cost(0, 0, 300_000),
    )(membership, jnp.transpose(prefix_cache, (1, 0, 2)), key_scale)
    prefix = gather_prefix(whole, membership, owners)
    w_far = across(w_out, 2)
    q, kv = pl.pallas_call(
        lambda *refs: qkv_kernel(*refs, tile=256),
        out_shape=(shaped((heads, suf, lanes), BF16),) * 2,
        in_specs=[VMEM] * 5,
        out_specs=(VMEM, VMEM),
        scratch_shapes=[pltpu.VMEM((heads, 2 * lanes, width), BF16)],
        name="qkv",
        compiler_params=vmem(14),
        cost_estimate=cost(2 * suf * width * 3 * heads * size, 0, 10_000_000),
    )(rows, w_query.T, w_key.T, w_value.T, key_scale)
    acc = pl.pallas_call(
        lambda *refs: suffix_kernel(*refs, tile=256),
        out_shape=shaped((heads, suf, lanes), F32),
        in_specs=[SMEM, SMEM, VMEM, VMEM],
        out_specs=VMEM,
        name="suffix",
        compiler_params=vmem(10),
        cost_estimate=cost(4 * suf * suf * heads * lanes, suf * suf * heads, 10_000_000),
    )(lengths, flag, q, kv)
    w_core = across(w_out, 1)
    w_both = across(w_far, 1)
    prefix_rows = prefix.shape[1]
    part = width // 4
    rank = lax.axis_index("tp").astype(jnp.int32).reshape(1)
    chunk = suf // CHUNKS
    attended = []
    for c in range(CHUNKS):
        attended.append(
            pl.pallas_call(
                lambda *refs: attend_kernel(*refs, tile=256),
                grid=(1,),
                out_shape=shaped((chunk, heads * size), BF16),
                in_specs=[
                    SMEM,
                    pl.BlockSpec((heads, chunk, lanes), lambda i, c=c: (0, c, 0)),
                    pl.BlockSpec((heads, chunk, lanes), lambda i, c=c: (0, c, 0)),
                    VMEM,
                ],
                out_specs=pl.BlockSpec((chunk, heads * size), lambda i: (0, 0)),
                scratch_shapes=[pltpu.VMEM((heads, chunk, lanes), F32)],
                name="attend",
        compiler_params=vmem(14),
                cost_estimate=cost(4 * chunk * prefix_rows * heads * lanes, chunk * prefix_rows * heads, 8_000_000),
            )(flag, q, acc, prefix)
        )
    out = None
    for c in range(CHUNKS):
        far = across(attended[c], 2)
        core = across(attended[c], 1)
        both = across(attended[c], 3)
        operands = [lengths, rank, attended[c], core, far, both, w_out, w_core, w_far, w_both, rows, step_rates.reshape(1, width)]
        specs = [SMEM] * 2 + [VMEM] * 8 + [pl.BlockSpec((chunk, width), lambda i, c=c: (c, 0)), VMEM]
        aliases = {}
        if out is not None:
            aliases = {len(operands): 0}
            operands.append(out)
            specs.append(ANY)
        out = pl.pallas_call(
            lambda *refs, c=c: output_kernel(*refs, tile=256, start=c * chunk),
            grid=(1,),
            out_shape=shaped((part, suf), BF16),
            in_specs=specs,
            out_specs=pl.BlockSpec((part, chunk), lambda i, c=c: (0, c)),
            input_output_aliases=aliases,
            scratch_shapes=[pltpu.VMEM((chunk, width), F32)],
            name="output",
        compiler_params=vmem(20),
            cost_estimate=cost(2 * chunk * width * width, 0, 6_000_000),
        )(*operands)
    return out.T.reshape(1, suf, part)


def solution(mesh):
    in_specs = (
        P("req", None, None),
        P("req"),
        P("req"),
        P(),
        P("req", "tp", None),
        P(None, "tp"),
        P(None, "tp"),
        P(None, "tp"),
        P("tp", None),
        P("tp", None),
        P(),
    )
    out_specs = P("req", None, "tp")
    return jax.shard_map(local, mesh=mesh, in_specs=in_specs, out_specs=out_specs, check_vma=False)
```

```python
import math

import jax
import jax.numpy as jnp
import numpy as np
from jax import lax
from jax.experimental import pallas as pl
from jax.experimental.pallas import tpu as pltpu
from jax.sharding import PartitionSpec as P


F32 = jnp.float32
BF16 = jnp.bfloat16
LOG2E = math.log2(math.e)
EPS = 1e-06

NX, NZ, NY = 2, 8, 4


def add3(a, b):
    return ((a[0] + b[0]) % NX, (a[1] + b[1]) % NZ, (a[2] + b[2]) % NY)


def flat3(a):
    return a[0] * NZ * NY + a[1] * NY + a[2]


def unflat3(i):
    return (i // (NZ * NY), (i // NY) % NZ, i % NY)


def fetch(array, offset):
    pairs = [(flat3(add3(unflat3(i), offset)), i) for i in range(NX * NZ * NY)]
    return lax.ppermute(array, "req", pairs)


QUAD = ((0, 0, 0), (1, 0, 0), (0, 4, 0), (1, 4, 0))
HALVES = (
    dict(
        pool=((0, 0, 0), (0, 1, 0), (0, 7, 0), (0, 6, 0)),
        near=((0, 0, 1), (0, 0, 3), (0, 0, 2)),
        sends=((0, 0, 1), (0, 0, 3), (0, 0, 2)),
    ),
    dict(
        pool=((0, 0, 0), (0, 0, 1), (0, 0, 3), (0, 0, 2)),
        near=((0, 1, 0), (0, 7, 0), (0, 2, 0)),
        sends=((0, 1, 0), (0, 7, 0), (0, 2, 0), (0, 6, 0)),
    ),
)
CAP = 8
SMALL = 64
CHUNKS = 2


def minus3(a):
    return (-a[0] % NX, -a[1] % NZ, -a[2] % NY)


def place_table(half):
    pool = [add3(p, q) for p in half["pool"] for q in QUAD]
    order = [add3(n, m) for n in ((0, 0, 0),) + half["near"] for m in pool]
    assert sorted(flat3(m) for m in order) == list(range(64))
    table = np.zeros(64, np.int32)
    for place, m in enumerate(order):
        table[flat3(m)] = place
    return table


def member_spot(target):
    for n, half in enumerate(HALVES):
        for k, p in enumerate(half["pool"]):
            for b, q in enumerate(QUAD):
                if add3(p, q) == target:
                    return n, k, b
    raise ValueError(target)


def dot_t(a, b):
    return lax.dot_general(a, b, (((1,), (1,)), ((), ())), preferred_element_type=F32)


def pair_lanes(scale, fill):
    return jnp.concatenate([scale, jnp.full_like(scale, fill)], axis=1)


def lane_half(lanes):
    return lax.broadcasted_iota(jnp.int32, (1, lanes), 1) < lanes // 2


def prep_kernel(member_ref, block_ref, scale_ref, flag_ref, whole_ref):
    heads, rows, lanes = block_ref.shape
    size = lanes // 2
    first = lane_half(lanes)
    scale = scale_ref[...]
    bound = jnp.max(scale * scale) * (1.02 * LOG2E * math.sqrt(size))
    flag_ref[0] = (bound <= 60.0).astype(jnp.int32)
    for h in range(heads):
        wide = block_ref[h].astype(F32)
        mean = jnp.sum(jnp.where(first, wide * wide, 0.0), axis=-1, keepdims=True) * (1.0 / size)
        keys = wide * lax.rsqrt(mean + EPS) * pair_lanes(scale[h : h + 1], 1.0)
        whole_ref[h] = jnp.where(first, keys, wide).astype(BF16)
    whole_ref[heads] = jnp.full((rows, lanes), member_ref[0].astype(F32)).astype(BF16)


def qkv_kernel(hid_ref, wq_ref, wk_ref, wv_ref, scale_ref, q_ref, kv_ref, w_ref, *, tile):
    heads, suf, lanes = q_ref.shape
    size = lanes // 2
    first = lane_half(lanes)
    for h in range(heads):
        own = slice(h * size, (h + 1) * size)
        w_ref[h, :size] = wq_ref[own]
        w_ref[h, size : 2 * size] = jnp.zeros_like(wq_ref[own])
        w_ref[h, 2 * size : 3 * size] = wk_ref[own]
        w_ref[h, 3 * size :] = wv_ref[own]
    for h in range(heads):
        scale = scale_ref[h : h + 1]
        q_scale = pair_lanes(scale * (LOG2E / math.sqrt(size)), 0.0)
        k_scale = pair_lanes(scale, 1.0)
        for i in range(suf // tile):
            rows = slice(i * tile, (i + 1) * tile)
            both = dot_t(hid_ref[rows], w_ref[h])
            q, kv = both[:, :lanes], both[:, lanes:]
            q_mean = jnp.sum(q * q, axis=-1, keepdims=True) * (1.0 / size)
            k_mean = jnp.sum(jnp.where(first, kv * kv, 0.0), axis=-1, keepdims=True) * (1.0 / size)
            q_ref[h, rows] = (q * lax.rsqrt(q_mean + EPS) * q_scale).astype(BF16)
            keys = kv * lax.rsqrt(k_mean + EPS) * k_scale
            kv_ref[h, rows] = jnp.where(first, keys, kv).astype(BF16)


def suffix_kernel(len_ref, flag_ref, q_ref, kv_ref, acc_ref, *, tile):
    heads, suf, lanes = q_ref.shape
    first = lane_half(lanes)
    length = len_ref[0]
    safe = flag_ref[0] == 1

    @pl.when(safe)
    def _():
        qpos = lax.broadcasted_iota(jnp.int32, (tile, tile), 0)
        kpos = lax.broadcasted_iota(jnp.int32, (tile, tile), 1)
        masks = []
        for j in range(suf // tile):
            inside = kpos + j * tile < length
            masks.append((inside & (kpos <= qpos), inside))
        for h in range(heads):
            for i in range(suf // tile):
                rows = slice(i * tile, (i + 1) * tile)
                total = None
                for j in range(i + 1):
                    keys = kv_ref[h, j * tile : (j + 1) * tile]
                    weights = jnp.exp2(dot_t(q_ref[h, rows], keys))
                    weights = jnp.where(masks[j][0 if i == j else 1], weights, 0.0).astype(BF16)
                    ones_values = jnp.where(first, jnp.ones_like(keys), keys)
                    part = jnp.dot(weights, ones_values, preferred_element_type=F32)
                    total = part if total is None else total + part
                acc_ref[h, rows] = total

    @pl.when(jnp.logical_not(safe))
    def _():
        lane = lax.broadcasted_iota(jnp.int32, (1, lanes), 1)
        pieces = suf // SMALL

        def piece(n, carry):
            h = n // pieces
            row = pl.multiple_of((n % pieces) * SMALL, SMALL)
            rows = pl.ds(row, SMALL)
            qpos = lax.broadcasted_iota(jnp.int32, (SMALL, suf), 0) + row
            kpos = lax.broadcasted_iota(jnp.int32, (SMALL, suf), 1)
            keys = kv_ref[h]
            scores = jnp.where((kpos <= qpos) & (kpos < length), dot_t(q_ref[h, rows], keys), -1e30)
            peak = jnp.max(scores, axis=-1, keepdims=True)
            weights = jnp.exp2(scores - peak).astype(BF16)
            ones_values = jnp.where(first, jnp.ones_like(keys), keys)
            total = jnp.dot(weights, ones_values, preferred_element_type=F32)
            acc_ref[h, rows] = jnp.where(lane == 0, peak, total)
            return carry

        lax.fori_loop(0, heads * pieces, piece, 0)


def split_kernel(a_ref, b_ref, c_ref, d_ref, one_ref, two_ref):
    rows = one_ref.shape[2]
    for n, ref in enumerate((a_ref, b_ref, c_ref, d_ref)):
        one_ref[n] = ref[:, :rows]
        two_ref[n] = ref[:, rows:]


def plan_kernel(member_ref, place_ref, owners_ref, table_ref, send_ref, recv_ref, over_ref, count_ref):
    group = member_ref[0]
    me = place_ref[0]
    groups, slots = owners_ref.shape

    def spots(owner):
        rel = (
            ((owner ^ me) & 32)
            + ((((owner >> 2) - (me >> 2)) & 7) << 2)
            + ((owner - me) & 3)
        )
        return table_ref[rel], table_ref[64 + rel]

    def by_group(g, most):
        for n in range(8):
            count_ref[n] = 0

        def by_slot(j, carry):
            most, held = carry
            owner = owners_ref[g, j]
            after = []
            for half, (spot, color) in enumerate(zip(spots(owner), (owner & 3, (owner >> 2) & 3))):
                send_ref[half * 64 + g * slots + held[half]] = spot
                after.append(held[half] + (spot < 16).astype(jnp.int32))
                seen = count_ref[half * 4 + color] + 1
                count_ref[half * 4 + color] = seen
                most = jnp.maximum(most, seen)
            return most, tuple(after)

        return lax.fori_loop(0, slots, by_slot, (most, (jnp.int32(0), jnp.int32(0))))[0]

    most = lax.fori_loop(0, groups, by_group, jnp.int32(0))
    over_ref[0] = (most > CAP).astype(jnp.int32)
    for n in range(8):
        count_ref[n] = 0

    def by_own(j, carry):
        for half, spot in enumerate(spots(owners_ref[group, j])):
            source = spot >> 4
            rank = count_ref[half * 4 + source]
            count_ref[half * 4 + source] = rank + 1
            recv_ref[half * slots + j] = source * 16 + rank
        return carry

    lax.fori_loop(0, slots, by_own, 0)


def pack_kernel(member_ref, send_ref, *rest, start):
    quads, outs, pool_ref = (rest[:4], rest[4:8]), rest[8:-1], rest[-1]
    heads = pool_ref.shape[2]
    for half in range(2):
        for n in range(4):
            pool_ref[half, 4 * n : 4 * n + 4] = quads[half][n][:, :heads]

    def wanted(target):
        n, k, b = member_spot(target)
        value = quads[n][k][b, heads].astype(F32)
        return jnp.max(value).astype(jnp.int32)

    jobs = []
    place = 0
    for n, half in enumerate(HALVES):
        if start == 0:
            jobs.append((outs[place], n, member_ref[0], 0))
            place += 1
        for k, offset in enumerate(half["sends"]):
            out = outs[place]
            place += 1
            jobs.append((out, n, wanted(minus3(offset)), start + (out.shape[0] if k == 3 else 0)))
    for out, half, group, first in jobs:

        def copy(i, carry, out=out, half=half, group=group, first=first):
            spot = send_ref[half * 64 + group * 16 + first + i] & 15
            out[i] = pool_ref[half, spot]
            return carry

        lax.fori_loop(0, out.shape[0], copy, 0)


def select_kernel(recv_ref, *rest):
    kv_ref, sems = rest[-2:]
    blocks = rest[:-2]
    slots = recv_ref.shape[0] // 2
    part = kv_ref.shape[1] // (2 * slots)
    spots = []
    for start in range(0, CAP * (2 if len(blocks) > 9 else 1), CAP):
        for n, half in enumerate(HALVES):
            if start == 0:
                spots.append((n, 0, 0))
            for k in range(len(half["sends"])):
                spots.append((n, min(k, 2) + 1, start + (CAP // 2 if k == 3 else 0)))
    assert len(spots) == len(blocks)

    def begin(j, carry):
        for half in range(2):
            code = recv_ref[half * slots + j]
            row = pl.multiple_of((2 * j + half) * part, part)
            goal = kv_ref.at[:, pl.ds(row, part), :]
            for ref, (n, source, low) in zip(blocks, spots):
                if n != half:
                    continue
                least = source * 16 + low

                @pl.when((code >= least) & (code < least + ref.shape[0]))
                def _(ref=ref, least=least):
                    pltpu.make_async_copy(ref.at[code - least], goal, sems.at[2 * j + half]).start()

        return carry

    lax.fori_loop(0, slots, begin, 0)

    def finish(j, carry):
        row = pl.multiple_of(j * part, part)
        goal = kv_ref.at[:, pl.ds(row, part), :]
        pltpu.make_async_copy(blocks[0].at[0], goal, sems.at[j]).wait()
        return carry

    lax.fori_loop(0, 2 * slots, finish, 0)


def attend_kernel(flag_ref, q_ref, acc_ref, kv_ref, out_ref, total_ref, *, tile):
    heads, rows, lanes = q_ref.shape
    size = lanes // 2
    count = kv_ref.shape[1]
    first = lane_half(lanes)
    safe = flag_ref[0] == 1

    @pl.when(safe)
    def _():
        for h in range(heads):
            total = acc_ref[h]
            for j in range(count // tile):
                keys = kv_ref[h, j * tile : (j + 1) * tile]
                weights = jnp.exp2(dot_t(q_ref[h], keys)).astype(BF16)
                ones_values = jnp.where(first, jnp.ones_like(keys), keys)
                total = total + jnp.dot(weights, ones_values, preferred_element_type=F32)
            total_ref[h] = total

    @pl.when(jnp.logical_not(safe))
    def _():
        pieces = rows // SMALL

        def piece(n, carry):
            h = n // pieces
            part = pl.ds(pl.multiple_of((n % pieces) * SMALL, SMALL), SMALL)
            keys = kv_ref[h]
            held = acc_ref[h, part]
            near = held[:, :1]
            held = jnp.where(first, held[:, 1:2], held)
            scores = dot_t(q_ref[h, part], keys)
            peak = jnp.maximum(jnp.max(scores, axis=-1, keepdims=True), near)
            weights = jnp.exp2(scores - peak).astype(BF16)
            ones_values = jnp.where(first, jnp.ones_like(keys), keys)
            total = jnp.dot(weights, ones_values, preferred_element_type=F32)
            total_ref[h, part] = total + held * jnp.exp2(near - peak)
            return carry

        lax.fori_loop(0, heads * pieces, piece, 0)

    for h in range(heads):
        total = total_ref[h]
        value = total / pltpu.roll(total, size, 1)
        out_ref[:, h * size : (h + 1) * size] = value[:, size:].astype(BF16)


def output_kernel(
    len_ref, rank_ref, a0, a1, a2, a3, w0, w1, w2, w3, hid_ref, rate_ref, *rest, tile, start
):
    out_ref, moved_ref = rest[-2:]
    count, width = hid_ref.shape
    part = out_ref.shape[0]
    length = len_ref[0]
    rank = rank_ref[0]
    cols = [slice(n * tile, (n + 1) * tile) for n in range(width // tile)]
    square = None
    for col in cols:
        branch = jnp.dot(a0[...], w0[:, col], preferred_element_type=F32)
        for a, w in ((a1, w1), (a2, w2), (a3, w3)):
            branch += jnp.dot(a[...], w[:, col], preferred_element_type=F32)
        moved_ref[:, col] = branch
        part_square = jnp.sum(branch * branch, axis=-1, keepdims=True)
        square = part_square if square is None else square + part_square
    gain = lax.rsqrt(square * (1.0 / width) + EPS)
    square = None
    for col in cols:
        state = hid_ref[:, col].astype(F32)
        moved = state + rate_ref[:, col] * (moved_ref[:, col] * gain - state)
        moved_ref[:, col] = moved
        part_square = jnp.sum(moved * moved, axis=-1, keepdims=True)
        square = part_square if square is None else square + part_square
    norm = lax.rsqrt(square * (1.0 / width) + EPS)
    pos = lax.broadcasted_iota(jnp.int32, (count, 1), 0) + start
    for t in range(width // part):

        @pl.when(rank == t)
        def _(t=t):
            mine = moved_ref[:, t * part : (t + 1) * part]
            out_ref[...] = jnp.where(pos < length, mine * norm, 0.0).T.astype(BF16)


VMEM = pl.BlockSpec(memory_space=pltpu.VMEM)
SMEM = pl.BlockSpec(memory_space=pltpu.SMEM)
ANY = pl.BlockSpec(memory_space=pl.ANY)


def across(array, bit):
    return lax.ppermute(array, "tp", [(i, i ^ bit) for i in range(4)])


def shaped(shape, dtype):
    return jax.ShapeDtypeStruct(shape, dtype)


def vmem(mebibytes):
    return pltpu.CompilerParams(vmem_limit_bytes=mebibytes << 20)


def cost(flops, exps, moved):
    return pl.CostEstimate(flops=flops, transcendentals=exps, bytes_accessed=moved)


def gather_prefix(whole, membership, owners):
    planes, rows, lanes = whole.shape
    heads, part, slots = planes - 1, rows // 2, owners.shape[1]
    place = lax.axis_index("req").astype(jnp.int32).reshape(1)
    table = jnp.asarray(np.concatenate([place_table(half) for half in HALVES]))
    send, recv, over = pl.pallas_call(
        plan_kernel,
        out_shape=(shaped((128,), jnp.int32), shaped((2 * slots,), jnp.int32), shaped((1,), jnp.int32)),
        in_specs=[SMEM] * 4,
        out_specs=(SMEM,) * 3,
        scratch_shapes=[pltpu.SMEM((8,), jnp.int32)],
        name="plan",
        compiler_params=vmem(1),
        cost_estimate=cost(0, 0, 1_000_000),
    )(membership, place, owners, table)
    quads = pl.pallas_call(
        split_kernel,
        out_shape=(shaped((4, planes, part, lanes), BF16),) * 2,
        in_specs=[VMEM] * 4,
        out_specs=(VMEM, VMEM),
        name="split",
        compiler_params=vmem(2),
        cost_estimate=cost(0, 0, 600_000),
    )(whole, *[fetch(whole, offset) for offset in QUAD[1:]])
    held = []
    for quad, half in zip(quads, HALVES):
        held += [quad] + [fetch(quad, offset) for offset in half["pool"][1:]]

    def one_round(start):
        shapes, offsets = [], []
        for half in HALVES:
            if start == 0:
                shapes.append(16)
                offsets.append(None)
            for offset in half["sends"]:
                shapes.append(CAP // 2 if len(half["sends"]) == 4 and offset[1] in (2, 6) else CAP)
                offsets.append(offset)
        packed = pl.pallas_call(
            lambda *refs: pack_kernel(*refs, start=start),
            out_shape=tuple(shaped((n, heads, part, lanes), BF16) for n in shapes),
            in_specs=[SMEM] * 2 + [VMEM] * 8,
            out_specs=(VMEM,) * len(shapes),
            scratch_shapes=[pltpu.VMEM((2, 16, heads, part, lanes), BF16)],
            name="pack",
            compiler_params=vmem(8),
            cost_estimate=cost(0, 0, 4_000_000),
        )(membership, send, *held)
        return [a if o is None else fetch(a, o) for a, o in zip(packed, offsets)]

    def select(arrays):
        return pl.pallas_call(
            select_kernel,
            out_shape=shaped((heads, slots * rows, lanes), BF16),
            in_specs=[SMEM] + [ANY] * len(arrays),
            out_specs=VMEM,
            scratch_shapes=[pltpu.SemaphoreType.DMA((2 * slots,))],
            name="select",
            compiler_params=vmem(4),
            cost_estimate=cost(0, 0, 3_000_000),
        )(recv, *arrays)

    arrays = one_round(0)
    prefix = lax.cond(
        over[0] > 0,
        lambda: select(arrays + one_round(CAP)),
        lambda: select(arrays),
    )
    return prefix


def local(
    hidden,
    membership,
    lengths,
    owners,
    prefix_cache,
    w_query,
    w_key,
    w_value,
    key_scale,
    w_out,
    step_rates,
):
    _, suf, width = hidden.shape
    heads, size = key_scale.shape
    lanes = 2 * size
    slot_rows = prefix_cache.shape[0]
    rows = hidden.reshape(suf, width)
    flag, whole = pl.pallas_call(
        prep_kernel,
        out_shape=(shaped((1,), jnp.int32), shaped((heads + 1, slot_rows, lanes), BF16)),
        in_specs=[SMEM, VMEM, VMEM],
        out_specs=(SMEM, VMEM),
        name="prep",
        cost_estimate=cost(0, 0, 300_000),
    )(membership, jnp.transpose(prefix_cache, (1, 0, 2)), key_scale)
    prefix = gather_prefix(whole, membership, owners)
    w_far = across(w_out, 2)
    q, kv = pl.pallas_call(
        lambda *refs: qkv_kernel(*refs, tile=256),
        out_shape=(shaped((heads, suf, lanes), BF16),) * 2,
        in_specs=[VMEM] * 5,
        out_specs=(VMEM, VMEM),
        scratch_shapes=[pltpu.VMEM((heads, 2 * lanes, width), BF16)],
        name="qkv",
        compiler_params=vmem(14),
        cost_estimate=cost(2 * suf * width * 3 * heads * size, 0, 10_000_000),
    )(rows, w_query.T, w_key.T, w_value.T, key_scale)
    acc = pl.pallas_call(
        lambda *refs: suffix_kernel(*refs, tile=256),
        out_shape=shaped((heads, suf, lanes), F32),
        in_specs=[SMEM, SMEM, VMEM, VMEM],
        out_specs=VMEM,
        name="suffix",
        compiler_params=vmem(10),
        cost_estimate=cost(4 * suf * suf * heads * lanes, suf * suf * heads, 10_000_000),
    )(lengths, flag, q, kv)
    w_core = across(w_out, 1)
    w_both = across(w_far, 1)
    prefix_rows = prefix.shape[1]
    part = width // 4
    rank = lax.axis_index("tp").astype(jnp.int32).reshape(1)
    chunk = suf // CHUNKS
    attended = []
    for c in range(CHUNKS):
        attended.append(
            pl.pallas_call(
                lambda *refs: attend_kernel(*refs, tile=1024),
                grid=(1,),
                out_shape=shaped((chunk, heads * size), BF16),
                in_specs=[
                    SMEM,
                    pl.BlockSpec((heads, chunk, lanes), lambda i, c=c: (0, c, 0)),
                    pl.BlockSpec((heads, chunk, lanes), lambda i, c=c: (0, c, 0)),
                    VMEM,
                ],
                out_specs=pl.BlockSpec((chunk, heads * size), lambda i: (0, 0)),
                scratch_shapes=[pltpu.VMEM((heads, chunk, lanes), F32)],
                compiler_params=vmem(14),
                cost_estimate=cost(4 * chunk * prefix_rows * heads * lanes, chunk * prefix_rows * heads, 8_000_000),
            )(flag, q, acc, prefix)
        )
    out = None
    for c in range(CHUNKS):
        far = across(attended[c], 2)
        core = across(attended[c], 1)
        both = across(far, 1) if c == 0 else across(attended[c], 3)
        operands = [lengths, rank, attended[c], core, far, both, w_out, w_core, w_far, w_both, rows, step_rates.reshape(1, width)]
        specs = [SMEM] * 2 + [VMEM] * 8 + [pl.BlockSpec((chunk, width), lambda i, c=c: (c, 0)), VMEM]
        aliases = {}
        if out is not None:
            aliases = {len(operands): 0}
            operands.append(out)
            specs.append(ANY)
        out = pl.pallas_call(
            lambda *refs, c=c: output_kernel(*refs, tile=256, start=c * chunk),
            grid=(1,),
            out_shape=shaped((part, suf), BF16),
            in_specs=specs,
            out_specs=pl.BlockSpec((part, chunk), lambda i, c=c: (0, c)),
            input_output_aliases=aliases,
            scratch_shapes=[pltpu.VMEM((chunk, width), F32)],
            name="output",
        compiler_params=vmem(20),
            cost_estimate=cost(2 * chunk * width * width, 0, 6_000_000),
        )(*operands)
    return out.T.reshape(1, suf, part)


def solution(mesh):
    in_specs = (
        P("req", None, None),
        P("req"),
        P("req"),
        P(),
        P("req", "tp", None),
        P(None, "tp"),
        P(None, "tp"),
        P(None, "tp"),
        P("tp", None),
        P("tp", None),
        P(),
    )
    out_specs = P("req", None, "tp")
    return jax.shard_map(local, mesh=mesh, in_specs=in_specs, out_specs=out_specs, check_vma=False)
```

```python
import math

import jax
import jax.numpy as jnp
import numpy as np
from jax import lax
from jax.experimental import pallas as pl
from jax.experimental.pallas import tpu as pltpu
from jax.sharding import PartitionSpec as P


F32 = jnp.float32
BF16 = jnp.bfloat16
LOG2E = math.log2(math.e)
EPS = 1e-06

NX, NZ, NY = 2, 8, 4


def add3(a, b):
    return ((a[0] + b[0]) % NX, (a[1] + b[1]) % NZ, (a[2] + b[2]) % NY)


def flat3(a):
    return a[0] * NZ * NY + a[1] * NY + a[2]


def unflat3(i):
    return (i // (NZ * NY), (i // NY) % NZ, i % NY)


def fetch(array, offset):
    pairs = [(flat3(add3(unflat3(i), offset)), i) for i in range(NX * NZ * NY)]
    return lax.ppermute(array, "req", pairs)


QUAD = ((0, 0, 0), (1, 0, 0), (0, 4, 0), (1, 4, 0))
HALVES = (
    dict(
        pool=((0, 0, 0), (0, 1, 0), (0, 7, 0), (0, 6, 0)),
        near=((0, 0, 1), (0, 0, 3), (0, 0, 2)),
        sends=((0, 0, 1), (0, 0, 3), (0, 0, 2)),
    ),
    dict(
        pool=((0, 0, 0), (0, 0, 1), (0, 0, 3), (0, 0, 2)),
        near=((0, 1, 0), (0, 7, 0), (0, 2, 0)),
        sends=((0, 1, 0), (0, 7, 0), (0, 2, 0), (0, 6, 0)),
    ),
)
CAP = 8
SMALL = 64
CHUNKS = 2


def minus3(a):
    return (-a[0] % NX, -a[1] % NZ, -a[2] % NY)


def place_table(half):
    pool = [add3(p, q) for p in half["pool"] for q in QUAD]
    order = [add3(n, m) for n in ((0, 0, 0),) + half["near"] for m in pool]
    assert sorted(flat3(m) for m in order) == list(range(64))
    table = np.zeros(64, np.int32)
    for place, m in enumerate(order):
        table[flat3(m)] = place
    return table


def member_spot(target):
    for n, half in enumerate(HALVES):
        for k, p in enumerate(half["pool"]):
            for b, q in enumerate(QUAD):
                if add3(p, q) == target:
                    return n, k, b
    raise ValueError(target)


def dot_t(a, b):
    return lax.dot_general(a, b, (((1,), (1,)), ((), ())), preferred_element_type=F32)


def pair_lanes(scale, fill):
    return jnp.concatenate([scale, jnp.full_like(scale, fill)], axis=1)


def lane_half(lanes):
    return lax.broadcasted_iota(jnp.int32, (1, lanes), 1) < lanes // 2


def prep_kernel(member_ref, block_ref, scale_ref, flag_ref, whole_ref):
    heads, rows, lanes = block_ref.shape
    size = lanes // 2
    first = lane_half(lanes)
    scale = scale_ref[...]
    bound = jnp.max(scale * scale) * (1.02 * LOG2E * math.sqrt(size))
    flag_ref[0] = (bound <= 60.0).astype(jnp.int32)
    for h in range(heads):
        wide = block_ref[h].astype(F32)
        mean = jnp.sum(jnp.where(first, wide * wide, 0.0), axis=-1, keepdims=True) * (1.0 / size)
        keys = wide * lax.rsqrt(mean + EPS) * pair_lanes(scale[h : h + 1], 1.0)
        whole_ref[h] = jnp.where(first, keys, wide).astype(BF16)
    whole_ref[heads] = jnp.full((rows, lanes), member_ref[0].astype(F32)).astype(BF16)


def qkv_kernel(hid_ref, wq_ref, wk_ref, wv_ref, scale_ref, q_ref, kv_ref, w_ref, *, tile):
    heads, suf, lanes = q_ref.shape
    size = lanes // 2
    first = lane_half(lanes)
    for h in range(heads):
        own = slice(h * size, (h + 1) * size)
        w_ref[h, :size] = wq_ref[own]
        w_ref[h, size : 2 * size] = jnp.zeros_like(wq_ref[own])
        w_ref[h, 2 * size : 3 * size] = wk_ref[own]
        w_ref[h, 3 * size :] = wv_ref[own]
    for h in range(heads):
        scale = scale_ref[h : h + 1]
        q_scale = pair_lanes(scale * (LOG2E / math.sqrt(size)), 0.0)
        k_scale = pair_lanes(scale, 1.0)
        for i in range(suf // tile):
            rows = slice(i * tile, (i + 1) * tile)
            both = dot_t(hid_ref[rows], w_ref[h])
            q, kv = both[:, :lanes], both[:, lanes:]
            q_mean = jnp.sum(q * q, axis=-1, keepdims=True) * (1.0 / size)
            k_mean = jnp.sum(jnp.where(first, kv * kv, 0.0), axis=-1, keepdims=True) * (1.0 / size)
            q_ref[h, rows] = (q * lax.rsqrt(q_mean + EPS) * q_scale).astype(BF16)
            keys = kv * lax.rsqrt(k_mean + EPS) * k_scale
            kv_ref[h, rows] = jnp.where(first, keys, kv).astype(BF16)


def suffix_kernel(len_ref, flag_ref, q_ref, kv_ref, acc_ref, *, tile):
    heads, suf, lanes = q_ref.shape
    first = lane_half(lanes)
    length = len_ref[0]
    safe = flag_ref[0] == 1

    @pl.when(safe)
    def _():
        qpos = lax.broadcasted_iota(jnp.int32, (tile, tile), 0)
        kpos = lax.broadcasted_iota(jnp.int32, (tile, tile), 1)
        masks = []
        for j in range(suf // tile):
            inside = kpos + j * tile < length
            masks.append((inside & (kpos <= qpos), inside))
        for h in range(heads):
            for i in range(suf // tile):
                rows = slice(i * tile, (i + 1) * tile)
                total = None
                for j in range(i + 1):
                    keys = kv_ref[h, j * tile : (j + 1) * tile]
                    weights = jnp.exp2(dot_t(q_ref[h, rows], keys))
                    weights = jnp.where(masks[j][0 if i == j else 1], weights, 0.0).astype(BF16)
                    ones_values = jnp.where(first, jnp.ones_like(keys), keys)
                    part = jnp.dot(weights, ones_values, preferred_element_type=F32)
                    total = part if total is None else total + part
                acc_ref[h, rows] = total

    @pl.when(jnp.logical_not(safe))
    def _():
        lane = lax.broadcasted_iota(jnp.int32, (1, lanes), 1)
        pieces = suf // SMALL

        def piece(n, carry):
            h = n // pieces
            row = pl.multiple_of((n % pieces) * SMALL, SMALL)
            rows = pl.ds(row, SMALL)
            qpos = lax.broadcasted_iota(jnp.int32, (SMALL, suf), 0) + row
            kpos = lax.broadcasted_iota(jnp.int32, (SMALL, suf), 1)
            keys = kv_ref[h]
            scores = jnp.where((kpos <= qpos) & (kpos < length), dot_t(q_ref[h, rows], keys), -1e30)
            peak = jnp.max(scores, axis=-1, keepdims=True)
            weights = jnp.exp2(scores - peak).astype(BF16)
            ones_values = jnp.where(first, jnp.ones_like(keys), keys)
            total = jnp.dot(weights, ones_values, preferred_element_type=F32)
            acc_ref[h, rows] = jnp.where(lane == 0, peak, total)
            return carry

        lax.fori_loop(0, heads * pieces, piece, 0)


def split_kernel(a_ref, b_ref, c_ref, d_ref, one_ref, two_ref, pair_ref):
    rows = one_ref.shape[2]
    for n, ref in enumerate((a_ref, b_ref, c_ref, d_ref)):
        one_ref[n] = ref[:, :rows]
        if n < 2:
            pair_ref[n] = ref[:, :rows]
        two_ref[n] = ref[:, rows:]


def plan_kernel(member_ref, place_ref, owners_ref, table_ref, send_ref, recv_ref, over_ref, count_ref):
    group = member_ref[0]
    me = place_ref[0]
    groups, slots = owners_ref.shape

    def spots(owner):
        rel = (
            ((owner ^ me) & 32)
            + ((((owner >> 2) - (me >> 2)) & 7) << 2)
            + ((owner - me) & 3)
        )
        return table_ref[rel], table_ref[64 + rel]

    def by_group(g, most):
        for n in range(8):
            count_ref[n] = 0

        def by_slot(j, carry):
            most, held = carry
            owner = owners_ref[g, j]
            after = []
            for half, (spot, color) in enumerate(zip(spots(owner), (owner & 3, (owner >> 2) & 3))):
                send_ref[half * 64 + g * slots + held[half]] = spot
                after.append(held[half] + (spot < 16).astype(jnp.int32))
                seen = count_ref[half * 4 + color] + 1
                count_ref[half * 4 + color] = seen
                most = jnp.maximum(most, seen)
            return most, tuple(after)

        return lax.fori_loop(0, slots, by_slot, (most, (jnp.int32(0), jnp.int32(0))))[0]

    most = lax.fori_loop(0, groups, by_group, jnp.int32(0))
    over_ref[0] = (most > CAP).astype(jnp.int32)
    for n in range(8):
        count_ref[n] = 0

    def by_own(j, carry):
        for half, spot in enumerate(spots(owners_ref[group, j])):
            source = spot >> 4
            rank = count_ref[half * 4 + source]
            count_ref[half * 4 + source] = rank + 1
            recv_ref[half * slots + j] = source * 16 + rank
        return carry

    lax.fori_loop(0, slots, by_own, 0)


def pack_kernel(member_ref, send_ref, *rest, start):
    pieces, outs, pool_ref = (rest[:5], rest[5:9]), rest[9:-1], rest[-1]
    heads = pool_ref.shape[2]
    blocks = []
    for half in range(2):
        held = [(ref, b) for ref in pieces[half] for b in range(ref.shape[0])]
        blocks.append(held)
        for n, (ref, b) in enumerate(held):
            pool_ref[half, n] = ref[b, :heads]

    def wanted(target):
        n, k, b = member_spot(target)
        ref, b = blocks[n][4 * k + b]
        value = ref[b, heads].astype(F32)
        return jnp.max(value).astype(jnp.int32)

    jobs = []
    place = 0
    for n, half in enumerate(HALVES):
        if start == 0:
            jobs.append((outs[place], n, member_ref[0], 0))
            place += 1
        for k, offset in enumerate(half["sends"]):
            out = outs[place]
            place += 1
            jobs.append((out, n, wanted(minus3(offset)), start + (out.shape[0] if k == 3 else 0)))
    for out, half, group, first in jobs:

        def copy(i, carry, out=out, half=half, group=group, first=first):
            spot = send_ref[half * 64 + group * 16 + first + i] & 15
            out[i] = pool_ref[half, spot]
            return carry

        lax.fori_loop(0, out.shape[0], copy, 0)


def select_kernel(recv_ref, *rest):
    kv_ref, sems = rest[-2:]
    blocks = rest[:-2]
    slots = recv_ref.shape[0] // 2
    part = kv_ref.shape[1] // (2 * slots)
    spots = []
    for start in range(0, CAP * (2 if len(blocks) > 9 else 1), CAP):
        for n, half in enumerate(HALVES):
            if start == 0:
                spots.append((n, 0, 0))
            for k in range(len(half["sends"])):
                spots.append((n, min(k, 2) + 1, start + (CAP // 2 if k == 3 else 0)))
    assert len(spots) == len(blocks)

    def begin(j, carry):
        for half in range(2):
            code = recv_ref[half * slots + j]
            row = pl.multiple_of((2 * j + half) * part, part)
            goal = kv_ref.at[:, pl.ds(row, part), :]
            for ref, (n, source, low) in zip(blocks, spots):
                if n != half:
                    continue
                least = source * 16 + low

                @pl.when((code >= least) & (code < least + ref.shape[0]))
                def _(ref=ref, least=least):
                    pltpu.make_async_copy(ref.at[code - least], goal, sems.at[2 * j + half]).start()

        return carry

    lax.fori_loop(0, slots, begin, 0)

    def finish(j, carry):
        row = pl.multiple_of(j * part, part)
        goal = kv_ref.at[:, pl.ds(row, part), :]
        pltpu.make_async_copy(blocks[0].at[0], goal, sems.at[j]).wait()
        return carry

    lax.fori_loop(0, 2 * slots, finish, 0)


def attend_kernel(flag_ref, q_ref, acc_ref, kv_ref, out_ref, total_ref, *, tile):
    heads, rows, lanes = q_ref.shape
    size = lanes // 2
    count = kv_ref.shape[1]
    first = lane_half(lanes)
    safe = flag_ref[0] == 1

    @pl.when(safe)
    def _():
        for h in range(heads):
            total = acc_ref[h]
            for j in range(count // tile):
                keys = kv_ref[h, j * tile : (j + 1) * tile]
                weights = jnp.exp2(dot_t(q_ref[h], keys)).astype(BF16)
                ones_values = jnp.where(first, jnp.ones_like(keys), keys)
                total = total + jnp.dot(weights, ones_values, preferred_element_type=F32)
            total_ref[h] = total

    @pl.when(jnp.logical_not(safe))
    def _():
        pieces = rows // SMALL

        def piece(n, carry):
            h = n // pieces
            part = pl.ds(pl.multiple_of((n % pieces) * SMALL, SMALL), SMALL)
            keys = kv_ref[h]
            held = acc_ref[h, part]
            near = held[:, :1]
            held = jnp.where(first, held[:, 1:2], held)
            scores = dot_t(q_ref[h, part], keys)
            peak = jnp.maximum(jnp.max(scores, axis=-1, keepdims=True), near)
            weights = jnp.exp2(scores - peak).astype(BF16)
            ones_values = jnp.where(first, jnp.ones_like(keys), keys)
            total = jnp.dot(weights, ones_values, preferred_element_type=F32)
            total_ref[h, part] = total + held * jnp.exp2(near - peak)
            return carry

        lax.fori_loop(0, heads * pieces, piece, 0)

    for h in range(heads):
        total = total_ref[h]
        value = total / pltpu.roll(total, size, 1)
        out_ref[:, h * size : (h + 1) * size] = value[:, size:].astype(BF16)


def output_kernel(
    len_ref, rank_ref, a0, a1, a2, a3, w0, w1, w2, w3, hid_ref, rate_ref, *rest, tile, start
):
    out_ref, moved_ref = rest[-2:]
    count, width = hid_ref.shape
    part = out_ref.shape[0]
    length = len_ref[0]
    rank = rank_ref[0]
    cols = [slice(n * tile, (n + 1) * tile) for n in range(width // tile)]
    square = None
    for col in cols:
        branch = jnp.dot(a0[...], w0[:, col], preferred_element_type=F32)
        for a, w in ((a1, w1), (a2, w2), (a3, w3)):
            branch += jnp.dot(a[...], w[:, col], preferred_element_type=F32)
        moved_ref[:, col] = branch
        part_square = jnp.sum(branch * branch, axis=-1, keepdims=True)
        square = part_square if square is None else square + part_square
    gain = lax.rsqrt(square * (1.0 / width) + EPS)
    square = None
    for col in cols:
        state = hid_ref[:, col].astype(F32)
        moved = state + rate_ref[:, col] * (moved_ref[:, col] * gain - state)
        moved_ref[:, col] = moved
        part_square = jnp.sum(moved * moved, axis=-1, keepdims=True)
        square = part_square if square is None else square + part_square
    norm = lax.rsqrt(square * (1.0 / width) + EPS)
    pos = lax.broadcasted_iota(jnp.int32, (count, 1), 0) + start
    for t in range(width // part):

        @pl.when(rank == t)
        def _(t=t):
            mine = moved_ref[:, t * part : (t + 1) * part]
            out_ref[...] = jnp.where(pos < length, mine * norm, 0.0).T.astype(BF16)


VMEM = pl.BlockSpec(memory_space=pltpu.VMEM)
SMEM = pl.BlockSpec(memory_space=pltpu.SMEM)
ANY = pl.BlockSpec(memory_space=pl.ANY)


def across(array, bit):
    return lax.ppermute(array, "tp", [(i, i ^ bit) for i in range(4)])


def shaped(shape, dtype):
    return jax.ShapeDtypeStruct(shape, dtype)


def vmem(mebibytes):
    return pltpu.CompilerParams(vmem_limit_bytes=mebibytes << 20)


def cost(flops, exps, moved):
    return pl.CostEstimate(flops=flops, transcendentals=exps, bytes_accessed=moved)


def gather_prefix(whole, membership, owners):
    planes, rows, lanes = whole.shape
    heads, part, slots = planes - 1, rows // 2, owners.shape[1]
    place = lax.axis_index("req").astype(jnp.int32).reshape(1)
    table = jnp.asarray(np.concatenate([place_table(half) for half in HALVES]))
    send, recv, over = pl.pallas_call(
        plan_kernel,
        out_shape=(shaped((128,), jnp.int32), shaped((2 * slots,), jnp.int32), shaped((1,), jnp.int32)),
        in_specs=[SMEM] * 4,
        out_specs=(SMEM,) * 3,
        scratch_shapes=[pltpu.SMEM((8,), jnp.int32)],
        name="plan",
        compiler_params=vmem(1),
        cost_estimate=cost(0, 0, 1_000_000),
    )(membership, place, owners, table)
    *quads, pair = pl.pallas_call(
        split_kernel,
        out_shape=tuple(shaped((n, planes, part, lanes), BF16) for n in (4, 4, 2)),
        in_specs=[VMEM] * 4,
        out_specs=(VMEM,) * 3,
        name="split",
        compiler_params=vmem(2),
        cost_estimate=cost(0, 0, 600_000),
    )(whole, *[fetch(whole, offset) for offset in QUAD[1:]])
    held = []
    for n, (quad, half) in enumerate(zip(quads, HALVES)):
        held.append(quad)
        for i, offset in enumerate(half["pool"][1:]):
            if n == 0 and i == 2:
                held.append(fetch(pair, offset))
                held.append(fetch(pair, add3(offset, QUAD[2])))
            else:
                held.append(fetch(quad, offset))

    def one_round(start):
        shapes, offsets = [], []
        for half in HALVES:
            if start == 0:
                shapes.append(16)
                offsets.append(None)
            for offset in half["sends"]:
                shapes.append(CAP // 2 if len(half["sends"]) == 4 and offset[1] in (2, 6) else CAP)
                offsets.append(offset)
        packed = pl.pallas_call(
            lambda *refs: pack_kernel(*refs, start=start),
            out_shape=tuple(shaped((n, heads, part, lanes), BF16) for n in shapes),
            in_specs=[SMEM] * 2 + [VMEM] * 9,
            out_specs=(VMEM,) * len(shapes),
            scratch_shapes=[pltpu.VMEM((2, 16, heads, part, lanes), BF16)],
            name="pack",
            compiler_params=vmem(8),
            cost_estimate=cost(0, 0, 4_000_000),
        )(membership, send, *held)
        return [a if o is None else fetch(a, o) for a, o in zip(packed, offsets)]

    def select(arrays):
        return pl.pallas_call(
            select_kernel,
            out_shape=shaped((heads, slots * rows, lanes), BF16),
            in_specs=[SMEM] + [ANY] * len(arrays),
            out_specs=VMEM,
            scratch_shapes=[pltpu.SemaphoreType.DMA((2 * slots,))],
            name="select",
            compiler_params=vmem(4),
            cost_estimate=cost(0, 0, 3_000_000),
        )(recv, *arrays)

    arrays = one_round(0)
    prefix = lax.cond(
        over[0] > 0,
        lambda: select(arrays + one_round(CAP)),
        lambda: select(arrays),
    )
    return prefix


def local(
    hidden,
    membership,
    lengths,
    owners,
    prefix_cache,
    w_query,
    w_key,
    w_value,
    key_scale,
    w_out,
    step_rates,
):
    _, suf, width = hidden.shape
    heads, size = key_scale.shape
    lanes = 2 * size
    slot_rows = prefix_cache.shape[0]
    rows = hidden.reshape(suf, width)
    flag, whole = pl.pallas_call(
        prep_kernel,
        out_shape=(shaped((1,), jnp.int32), shaped((heads + 1, slot_rows, lanes), BF16)),
        in_specs=[SMEM, VMEM, VMEM],
        out_specs=(SMEM, VMEM),
        name="prep",
        cost_estimate=cost(0, 0, 300_000),
    )(membership, jnp.transpose(prefix_cache, (1, 0, 2)), key_scale)
    prefix = gather_prefix(whole, membership, owners)
    w_far = across(w_out, 2)
    q, kv = pl.pallas_call(
        lambda *refs: qkv_kernel(*refs, tile=256),
        out_shape=(shaped((heads, suf, lanes), BF16),) * 2,
        in_specs=[VMEM] * 5,
        out_specs=(VMEM, VMEM),
        scratch_shapes=[pltpu.VMEM((heads, 2 * lanes, width), BF16)],
        name="qkv",
        compiler_params=vmem(14),
        cost_estimate=cost(2 * suf * width * 3 * heads * size, 0, 10_000_000),
    )(rows, w_query.T, w_key.T, w_value.T, key_scale)
    acc = pl.pallas_call(
        lambda *refs: suffix_kernel(*refs, tile=256),
        out_shape=shaped((heads, suf, lanes), F32),
        in_specs=[SMEM, SMEM, VMEM, VMEM],
        out_specs=VMEM,
        name="suffix",
        compiler_params=vmem(10),
        cost_estimate=cost(4 * suf * suf * heads * lanes, suf * suf * heads, 10_000_000),
    )(lengths, flag, q, kv)
    w_core = across(w_out, 1)
    w_both = across(w_far, 1)
    prefix_rows = prefix.shape[1]
    part = width // 4
    rank = lax.axis_index("tp").astype(jnp.int32).reshape(1)
    chunk = suf // CHUNKS
    attended = []
    for c in range(CHUNKS):
        attended.append(
            pl.pallas_call(
                lambda *refs: attend_kernel(*refs, tile=1024),
                grid=(1,),
                out_shape=shaped((chunk, heads * size), BF16),
                in_specs=[
                    SMEM,
                    pl.BlockSpec((heads, chunk, lanes), lambda i, c=c: (0, c, 0)),
                    pl.BlockSpec((heads, chunk, lanes), lambda i, c=c: (0, c, 0)),
                    VMEM,
                ],
                out_specs=pl.BlockSpec((chunk, heads * size), lambda i: (0, 0)),
                scratch_shapes=[pltpu.VMEM((heads, chunk, lanes), F32)],
                compiler_params=vmem(14),
                cost_estimate=cost(4 * chunk * prefix_rows * heads * lanes, chunk * prefix_rows * heads, 8_000_000),
            )(flag, q, acc, prefix)
        )
    out = None
    for c in range(CHUNKS):
        far = across(attended[c], 2)
        core = across(attended[c], 1)
        both = across(far, 1)
        operands = [lengths, rank, attended[c], core, far, both, w_out, w_core, w_far, w_both, rows, step_rates.reshape(1, width)]
        specs = [SMEM] * 2 + [VMEM] * 8 + [pl.BlockSpec((chunk, width), lambda i, c=c: (c, 0)), VMEM]
        aliases = {}
        if out is not None:
            aliases = {len(operands): 0}
            operands.append(out)
            specs.append(ANY)
        out = pl.pallas_call(
            lambda *refs, c=c: output_kernel(*refs, tile=256, start=c * chunk),
            grid=(1,),
            out_shape=shaped((part, suf), BF16),
            in_specs=specs,
            out_specs=pl.BlockSpec((part, chunk), lambda i, c=c: (0, c)),
            input_output_aliases=aliases,
            scratch_shapes=[pltpu.VMEM((chunk, width), F32)],
            compiler_params=vmem(20),
            cost_estimate=cost(2 * chunk * width * width, 0, 6_000_000),
        )(*operands)
    return out.T.reshape(1, suf, part)


def solution(mesh):
    in_specs = (
        P("req", None, None),
        P("req"),
        P("req"),
        P(),
        P("req", "tp", None),
        P(None, "tp"),
        P(None, "tp"),
        P(None, "tp"),
        P("tp", None),
        P("tp", None),
        P(),
    )
    out_specs = P("req", None, "tp")
    return jax.shard_map(local, mesh=mesh, in_specs=in_specs, out_specs=out_specs, check_vma=False)
```
